256 devices in a mesh: gene: 4 (over x), sample: 16 (over y, z_lo, core), variant: 4 (over z_hi).
Axes of the slice: x: 4, y: 4, z: 8 (z_hi: 4, z_lo: 2; z = z_hi * 2 + z_lo), core: 2. Of those that a mesh axis runs over, the one named last changes fastest.
Arguments:
- expression: bfloat16 [65536, 4096], P('sample', 'gene'), may hold values from -6 to 6
- profile: float32 [4096, 7], P('gene'), may hold values from -0.25 to 0.25
- dosage: int32 [65536, 512], P('sample', 'variant'), may hold values from 0 to 2
- signature: int32 [500], replicated, may hold values from 0 to 4095, as said below
Outputs:
- interaction: float32 [3584, 4096], P(('variant', 'sample'), 'gene')
- proportions: float32 [65536, 7], P('sample')
The draws below stay inside these ranges and needn't reach their ends.
Inputs may be any that keep to these rules, and one draw needn't show every extreme that they name: `signature`: distinct gene indices; gene 0 and gene 4096 - 1 are always among them.
All inputs are finite; a program needn't handle non-finite values.
Results may differ from the reference program's by a relative error of at most 0.0045.
Values sent between devices are 32-bit elements; how exact they have to be, the bound alone decides.
A program may use at most 128 MiB of HBM per device.

```python
import math
import jax
import jax.numpy as jnp
from jax import lax

GENES = 4096
SIG = 500
K = 7
V_DEV = 128
SAMPLES = 65536
VARIANTS = 512
N_VARIANT = 4


def draw_signature(key, part):
    first = jax.random.permutation(jax.random.fold_in(key, 11), GENES - 2)[:SIG - 2] + 1
    joined = jnp.concatenate([jnp.array([0, GENES - 1], jnp.int32), first.astype(jnp.int32)])
    order = jax.random.permutation(jax.random.fold_in(key, 12), SIG)
    return joined[order].astype(jnp.int32)


def place_ends(result, own_key, smallest, largest):
    shape = result.shape
    place = [jax.random.randint(jax.random.fold_in(own_key, axis), (), 0, shape[axis]) for axis in range(len(shape))]
    result = result.at[tuple(place)].set(smallest)
    longest = shape.index(max(shape))
    place[longest] = (place[longest] + 1) % shape[longest]
    return result.at[tuple(place)].set(largest)


def shard_levels(rng, dims, pieces, smallest, high):
    gain = 1.0
    for position, blocks in pieces:
        heights = jax.random.uniform(jax.random.fold_in(jax.random.fold_in(rng, 6), position), (blocks,), jnp.float32, smallest / len(pieces), high / len(pieces))
        gain = gain * jnp.repeat(jnp.exp(heights), dims[position] // blocks).reshape((-1,) + (1,) * (len(dims) - 1 - position))
    return gain


def normal_values(own_key, extent, width, reach, shards=(), kind=jnp.bfloat16):
    result = jax.random.normal(own_key, extent, jnp.float32) * width
    if len(shards) > 0:
        result = shard_levels(own_key, extent, shards, -0.22, 0.18) * result
    return jnp.clip(result, min=-reach, max=reach).astype(kind)


def setup_inputs(seed: int = 0) -> dict:
    seeds = jax.random.split(jax.random.key(seed), 5)
    return {
        "expression": normal_values(seeds[0], (SAMPLES, GENES), 1.0, 6.0, ((0, 16), (1, 4))),
        "profile": normal_values(seeds[1], (GENES, K), SIG ** -0.5, 0.25, ((0, 4),), jnp.float32),
        "dosage": place_ends(jax.random.randint(seeds[2], (SAMPLES, VARIANTS), 0, 3), jax.random.fold_in(seeds[2], 1), 0, 2).astype(jnp.int32),
        "signature": draw_signature(jax.random.fold_in(seeds[4], 71), 0),
    }


def chol_solve(gram, rhs):
    factor = jnp.linalg.cholesky(gram)
    return jax.scipy.linalg.cho_solve((factor, True), rhs)

def reference(expression, profile, dosage, signature):
    high = lax.Precision.HIGHEST
    member = jnp.zeros((GENES,), jnp.float32).at[signature].set(1.0)
    masked = profile * member[:, None]
    gram = jnp.dot(masked.T, masked, precision=high)
    floats = expression.astype(jnp.float32)
    rhs = jnp.dot(masked.T, floats.T, precision=high)
    props_t = chol_solve(gram, rhs)
    props = props_t.T
    pp_mat = jnp.dot(props_t, props, precision=high)
    py_mat = jnp.dot(props_t, floats, precision=high)
    coef = chol_solve(pp_mat, py_mat)
    rounded = props.astype(jnp.bfloat16).astype(jnp.float32)
    dos_float = dosage.astype(jnp.float32)
    weights = (rounded[:, :, None] * props[:, None, :]).reshape(SAMPLES, K * K)

    def block(index):
        piece = lax.dynamic_slice_in_dim(dos_float, (index * V_DEV).astype(jnp.int32), V_DEV, 1)
        design = (piece[:, :, None] * rounded[:, None, :]).reshape(SAMPLES, V_DEV * K)
        cross = jnp.dot(design.T, floats, precision=high)
        corr = jnp.dot(piece.T, weights, precision=high).reshape(V_DEV * K, K)
        return cross - jnp.dot(corr, coef, precision=high)
    parts = lax.map(block, jnp.arange(N_VARIANT, dtype=jnp.int32))
    scale = jnp.float32(1.0 / math.sqrt(SAMPLES))
    interaction = parts.reshape(VARIANTS * K, GENES) * scale
    return (interaction, props)
```

```python
import functools
import math

import jax
import jax.numpy as jnp
from jax import lax
from jax.experimental import pallas as pl
from jax.experimental.pallas import tpu as pltpu
from jax.sharding import PartitionSpec as P

MESH = pl.DeviceIdType.MESH
HIGH = lax.Precision.HIGHEST
F32, BF16 = jnp.float32, jnp.bfloat16
NT = (((1,), (1,)), ((), ()))
N_GENE = 4
N_SAMPLE = 16
N_CHUNK = 4
PARTS = ((0, 2, "abz"), (2, 4, "zab"), (4, 7, "bza"))


def ldl(gram):
    row = lax.broadcasted_iota(jnp.int32, (8, 8), 0)
    col = lax.broadcasted_iota(jnp.int32, (8, 8), 1)
    eye = (row == col).astype(F32)
    a = jnp.where((row == 7) | (col == 7), eye, gram)
    inv, inv_t = eye, eye
    for j in range(6):
        piv = a[j : j + 1, j : j + 1]
        f_col = jnp.where(row[:, :1] > j, a[:, j : j + 1] / piv, 0.0)
        f_row = jnp.where(col[:1, :] > j, a[j : j + 1, :] / piv, 0.0)
        inv = inv - f_col * inv[j : j + 1, :]
        inv_t = inv_t - inv_t[:, j : j + 1] * f_row
        a = a - f_col * a[j : j + 1, :]
    diag = jnp.sum(a * eye, axis=1, keepdims=True)
    return inv, inv_t, diag


def solve(factor, rhs):
    inv, inv_t, diag = factor
    mid = inv[:, 0:1] * rhs[0:1, :]
    for j in range(1, 7):
        mid = mid + inv[:, j : j + 1] * rhs[j : j + 1, :]
    mid = mid / diag
    out = inv_t[:, 0:1] * mid[0:1, :]
    for j in range(1, 7):
        out = out + inv_t[:, j : j + 1] * mid[j : j + 1, :]
    return out


def kernel(
    scale,
    sig_ref, prof_ref, expr_hbm, dos_hbm,
    inter_ref, props_ref,
    e_v, d_v, d_t, des, w_hi, w_lo, sig_sc, m_sc, acc, rc, r1, r2, r3, facc,
    pbuf, rsnd, rrcv, gsnd, grcv, corr_sc, pp_sc, tsrc, trcv, tbuf, mix,
    e_sem, d_sem, g_s, g_r, x_s, x_r, p_s, p_r, c_s, c_r, h_s, h_r, t_s, t_r, u_s, u_r,
):
    s_dev, g_dev = e_v.shape
    quarter = s_dev // N_GENE
    half = quarter // 2
    n_cols = g_dev // N_CHUNK
    types = 7
    g = lax.axis_index("gene")
    s = lax.axis_index("sample")
    y, z, c = s // 4, (s // 2) % 2, s % 2
    b = y // 2
    a = (y + b) % 2
    place = {"a": a, "b": b, "z": z}
    other = {
        "a": (2 * b + (1 - a + b) % 2) * 4 + z * 2 + c,
        "b": (2 * (1 - b) + (a + 1 - b) % 2) * 4 + z * 2 + c,
        "z": s + 2 - 4 * z,
    }
    core = s + 1 - 2 * c

    def gene_of(d):
        return {"gene": (g + d) % N_GENE}

    def sample_of(d):
        return {"sample": (s + d) % N_SAMPLE}

    def load(d, h):
        rows = pl.ds(pl.multiple_of(((g + d) % N_GENE) * quarter + h * half, half), half)
        return pltpu.make_async_copy(expr_hbm.at[rows, :], e_v.at[rows, :], e_sem.at[d, h])

    def remote(src, dst, send, recv, device):
        return pltpu.make_async_remote_copy(
            src_ref=src, dst_ref=dst, send_sem=send, recv_sem=recv, device_id=device, device_id_type=MESH
        )

    order = (2, 1, 3, 0)
    for d in order:
        for h in range(2):
            load(d, h).start()
    dos_copy = pltpu.make_async_copy(dos_hbm, d_v, d_sem)
    dos_copy.start()

    barrier = pltpu.get_barrier_semaphore()
    for d in range(1, N_GENE):
        pl.semaphore_signal(barrier, inc=1, device_id=gene_of(d), device_id_type=MESH)
    for d in range(1, N_SAMPLE):
        pl.semaphore_signal(barrier, inc=1, device_id=sample_of(d), device_id_type=MESH)

    n_sig = sig_ref.shape[1]
    sig_sc[...] = jnp.full(sig_sc.shape, -1, jnp.int32)
    sig_sc[0:1, 0:n_sig] = sig_ref[...]
    cols = []
    for t in range(sig_sc.shape[1] // 128):
        line = sig_sc[0:1, 128 * t : 128 * t + 128].astype(F32)
        cols.append(jnp.transpose(jnp.broadcast_to(line, (128, 128))))
    lane = lax.broadcasted_iota(jnp.int32, (128, 128), 1) + g * g_dev
    m_sc[...] = jnp.zeros(m_sc.shape, F32)
    for t in range(g_dev // 128):
        ids = (lane + 128 * t).astype(F32)
        hit = jnp.zeros((128, 128), F32)
        for column in cols:
            hit = jnp.where(column == ids, 1.0, hit)
        member = jnp.max(hit, axis=0, keepdims=True)
        m_sc[0:types, 128 * t : 128 * t + 128] = prof_ref[:, 128 * t : 128 * t + 128] * member
    masked = m_sc[...]
    gsnd[...] = jnp.zeros(gsnd.shape, F32)
    gsnd[:, 0:8] = lax.dot_general(masked, masked, NT, precision=HIGH, preferred_element_type=F32)
    top = masked.astype(BF16).astype(F32)
    rest = masked - top
    mid = rest.astype(BF16).astype(F32)
    m3 = jnp.concatenate([top, mid, rest - mid], axis=0).astype(BF16)

    pl.semaphore_wait(barrier, N_GENE - 1 + N_SAMPLE - 1)

    def gram_copy(d):
        return remote(gsnd, grcv.at[d - 1], g_s.at[d - 1], g_r.at[d - 1], gene_of(d))

    def rhs_copy(d):
        return remote(rsnd.at[d], rrcv.at[d - 1], x_s.at[d - 1], x_r.at[d - 1], gene_of(d))

    for d in range(1, N_GENE):
        gram_copy(d).start()
    for d in order:
        for h in range(2):
            load(d, h).wait()
            rows = pl.ds(pl.multiple_of(((g + d) % N_GENE) * quarter + h * half, half), half)
            part = lax.dot_general(m3, e_v[rows, :], NT, preferred_element_type=F32)
            rsnd[d, :, h * half : (h + 1) * half] = part[0:8] + part[8:16] + part[16:24]
        if d:
            rhs_copy(d).start()

    dos_copy.wait()

    def turn(i, carry):
        rows = pl.ds(pl.multiple_of(i * 128, 128), 128)
        d_t[:, rows] = jnp.transpose(d_v[rows, :].astype(F32)).astype(BF16)
        return carry

    lax.fori_loop(0, s_dev // 128, turn, 0)
    gram = gsnd[:, 0:8]
    for d in range(1, N_GENE):
        gram_copy(d).wait_recv()
        gram = gram + grcv[d - 1, :, 0:8]
    factor = ldl(gram)
    rhs = rsnd[0]
    for d in (1, 3, 2):
        rhs_copy(d).wait_recv()
        rhs = rhs + rrcv[d - 1]
    pbuf[g] = solve(factor, rhs)

    def props_copy(d):
        return remote(pbuf.at[g], pbuf.at[g], p_s.at[d - 1], p_r.at[d - 1], gene_of(d))

    for d in (2, 1, 3):
        props_copy(d).start()

    corr_sc[...] = jnp.zeros(corr_sc.shape, F32)
    pp_sc[...] = jnp.zeros(pp_sc.shape, F32)
    for d in (0, 1, 3, 2):
        if d:
            props_copy(d).wait_recv()
        q = (g + N_GENE - d) % N_GENE
        span = pl.ds(pl.multiple_of(q * quarter, quarter), quarter)
        props = pbuf[q]
        props_ref[:, span] = props[0:types]
        top = props.astype(BF16).astype(F32)
        des[896:912, span] = jnp.concatenate([top, props - top], axis=0).astype(BF16)
        highs, lows = [], []
        for k in range(types):
            wide = jnp.broadcast_to(top[k : k + 1, :], (16, quarter)).astype(BF16)
            for bb in range(2):
                for aa in range(2):
                    for zz in range(2):
                        source = ((2 * bb + (aa + bb) % 2) * 2 + zz) * 16
                        target = (((bb * 2 + aa) * 2 + zz) * types + k) * 16
                        des[target : target + 16, span] = d_t[source : source + 16, span] * wide
            weight = jnp.broadcast_to(top[k : k + 1, :], (8, quarter)) * props
            high = weight.astype(BF16).astype(F32)
            highs.append(high)
            lows.append(weight - high)
        w_hi[...] = jnp.concatenate(highs, axis=0).astype(BF16)
        w_lo[...] = jnp.concatenate(lows, axis=0).astype(BF16)
        turned = d_t[:, span]
        corr_sc[:, 0:56] += lax.dot_general(
            turned, w_hi[...], NT, preferred_element_type=F32
        ) + lax.dot_general(turned, w_lo[...], NT, preferred_element_type=F32)
        pp_sc[:, 0:8] += lax.dot_general(props, props, NT, precision=HIGH, preferred_element_type=F32)

    def core_copy(n):
        return remote(
            acc.at[n, :, :, :, :, 1 - c], rc.at[n], c_s.at[n], c_r.at[n], {"sample": core}
        )

    def block(n, ks, fixed):
        at = tuple(fixed.get(axis, slice(None)) for axis in "baz")
        return (n,) + at + (ks, c)

    def halving(n, part, step):
        lo, hi, axes = PARTS[part]
        ks = slice(lo, hi)
        kept = {axis: place[axis] for axis in axes[:step]}
        axis = axes[step]
        landing = ((r1, r2, r3)[step])[part].at[n]
        copy = remote(
            acc.at[block(n, ks, {**kept, axis: 1 - place[axis]})],
            landing,
            h_s.at[n, part, step],
            h_r.at[n, part, step],
            {"sample": other[axis]},
        )
        return copy, block(n, ks, {**kept, axis: place[axis]}), landing

    def tile_copy(d):
        return remote(tsrc.at[(s + d) % N_SAMPLE], trcv.at[d - 1], t_s.at[d - 1], t_r.at[d - 1], sample_of(d))

    def spread_copy(d):
        return remote(tbuf.at[s], tbuf.at[s], u_s.at[d - 1], u_r.at[d - 1], sample_of(d))

    def stage(t, carry):
        @pl.when(t < N_CHUNK)
        def _():
            columns = pl.ds(pl.multiple_of(t * n_cols, n_cols), n_cols)
            shape = acc.shape[1:]

            def term(q):
                span = pl.ds(pl.multiple_of(q * quarter, quarter), quarter)
                return jnp.dot(des[:, span], e_v[span, columns], preferred_element_type=F32)

            def put(value, first):
                body, tail = value[0:896].reshape(shape), value[896:904] + value[904:912]
                for i in range(n_cols // 128):
                    piece = tail[:, 128 * i : 128 * i + 128]
                    at = t * (n_cols // 128) + i
                    tsrc[at, 1] = piece if first else tsrc[at, 1] + piece
                acc[t] = body if first else acc[t] + body

            put(term(0), True)

            def more(q, carry):
                put(term(q), False)
                return carry

            lax.fori_loop(1, N_GENE, more, 0)
            core_copy(t).start()

        @pl.when((t >= 1) & (t < N_CHUNK + 1))
        def _():
            n = t - 1
            core_copy(n).wait_recv()
            acc[n, :, :, :, :, c] += rc[n]
            for part in range(3):
                halving(n, part, 0)[0].start()

        for step in range(3):
            @pl.when((t >= 2 + step) & (t < N_CHUNK + 2 + step))
            def _(step=step):
                n = t - 2 - step
                for part in range(3):
                    copy, kept, landing = halving(n, part, step)
                    copy.wait_recv()
                    if step < 2:
                        acc[kept] += landing[...]
                        halving(n, part, step + 1)[0].start()
                    else:
                        lo, hi, _ = PARTS[part]
                        at = pl.ds(pl.multiple_of(n * n_cols, n_cols), n_cols)
                        facc[lo:hi, :, at] = acc[kept] + landing[...]

        @pl.when(t == N_CHUNK - 1)
        def _():
            for i in range(N_SAMPLE):
                tsrc[i, 0] = corr_sc[8 * i : 8 * i + 8, :]
            tsrc[g_dev // 128, 1] = pp_sc[...]
            for i in range(g_dev // 128 + 1, N_SAMPLE):
                tsrc[i, 1] = jnp.zeros((8, 128), F32)

            def send(d, carry):
                tile_copy(d).start()
                return carry

            lax.fori_loop(1, N_SAMPLE, send, 0)

        @pl.when(t == N_CHUNK + 1)
        def _():
            def take(d, carry):
                tile_copy(d).wait_recv()
                return carry + trcv[d - 1]

            total = lax.fori_loop(1, N_SAMPLE, take, tsrc[s])
            corr_sc[0:8, :] = total[0]
            tbuf[s] = total[1]

            def send(d, carry):
                spread_copy(d).start()
                return carry

            lax.fori_loop(1, N_SAMPLE, send, 0)

        return carry

    lax.fori_loop(0, N_CHUNK + 4, stage, 0)

    def gather(d, carry):
        spread_copy(d).wait_recv()
        return carry

    lax.fori_loop(1, N_SAMPLE, gather, 0)
    n_tiles = g_dev // 128
    py = jnp.concatenate([tbuf[i] for i in range(n_tiles)], axis=1)
    coef = solve(ldl(tbuf[n_tiles, :, 0:8]), py)
    corr = corr_sc[0:8, :]
    for k in range(types):
        value = facc[k]
        for j in range(types):
            value = value - corr[:, 8 * k + j : 8 * k + j + 1] * coef[j : j + 1, :]
        value = value * scale
        for i in range(n_tiles):
            mix[i, pl.ds(k, 8, stride=types), :] = value[:, 128 * i : 128 * i + 128]
    for i in range(n_tiles):
        inter_ref[:, 128 * i : 128 * i + 128] = mix[i]

    for d in range(1, N_GENE):
        gram_copy(d).wait_send()
        rhs_copy(d).wait_send()
        props_copy(d).wait_send()

    def drain(n, carry):
        core_copy(n).wait_send()
        for part in range(3):
            for step in range(3):
                halving(n, part, step)[0].wait_send()
        return carry

    lax.fori_loop(0, N_CHUNK, drain, 0)

    def drain_tiles(d, carry):
        tile_copy(d).wait_send()
        spread_copy(d).wait_send()
        return carry

    lax.fori_loop(1, N_SAMPLE, drain_tiles, 0)


def local(expression, profile, dosage, signature):
    s_dev, g_dev = expression.shape
    v_dev = dosage.shape[1]
    types = profile.shape[1]
    quarter, n_cols = s_dev // N_GENE, g_dev // N_CHUNK
    scale = 1.0 / math.sqrt(s_dev * N_SAMPLE)
    sig_cols = -(-signature.shape[0] // 128) * 128
    sizes = [hi - lo for lo, hi, _ in PARTS]
    vmem, dma = pltpu.VMEM, pltpu.SemaphoreType.DMA
    inter, props_t = pl.pallas_call(
        functools.partial(kernel, scale),
        out_shape=(
            jax.ShapeDtypeStruct((v_dev * types // N_SAMPLE, g_dev), F32),
            jax.ShapeDtypeStruct((types, s_dev), F32),
        ),
        in_specs=[
            pl.BlockSpec(memory_space=pltpu.VMEM),
            pl.BlockSpec(memory_space=pltpu.VMEM),
            pl.BlockSpec(memory_space=pl.ANY),
            pl.BlockSpec(memory_space=pl.ANY),
        ],
        out_specs=(pl.BlockSpec(memory_space=pltpu.VMEM), pl.BlockSpec(memory_space=pltpu.VMEM)),
        scratch_shapes=[
            vmem((s_dev, g_dev), BF16),
            vmem((s_dev, v_dev), jnp.int32),
            vmem((v_dev, s_dev), BF16),
            vmem((v_dev * types + 16, s_dev), BF16),
            vmem((8 * types, quarter), BF16),
            vmem((8 * types, quarter), BF16),
            vmem((1, sig_cols), jnp.int32),
            vmem((8, g_dev), F32),
            vmem((N_CHUNK, 2, 2, 2, types, 2, 8, n_cols), F32),
            vmem((N_CHUNK, 2, 2, 2, types, 8, n_cols), F32),
            [vmem((N_CHUNK, 2, 2, k, 8, n_cols), F32) for k in sizes],
            [vmem((N_CHUNK, 2, k, 8, n_cols), F32) for k in sizes],
            [vmem((N_CHUNK, k, 8, n_cols), F32) for k in sizes],
            vmem((types, 8, g_dev), F32),
            vmem((N_GENE, 8, quarter), F32),
            vmem((N_GENE, 8, quarter), F32),
            vmem((N_GENE - 1, 8, quarter), F32),
            vmem((8, 128), F32),
            vmem((N_GENE - 1, 8, 128), F32),
            vmem((v_dev, 128), F32),
            vmem((8, 128), F32),
            vmem((N_SAMPLE, 2, 8, 128), F32),
            vmem((N_SAMPLE - 1, 2, 8, 128), F32),
            vmem((N_SAMPLE, 8, 128), F32),
            vmem((g_dev // 128, 8 * types, 128), F32),
            dma((N_GENE, 2)),
            dma,
            dma((N_GENE - 1,)),
            dma((N_GENE - 1,)),
            dma((N_GENE - 1,)),
            dma((N_GENE - 1,)),
            dma((N_GENE - 1,)),
            dma((N_GENE - 1,)),
            dma((N_CHUNK,)),
            dma((N_CHUNK,)),
            dma((N_CHUNK, 3, 3)),
            dma((N_CHUNK, 3, 3)),
            dma((N_SAMPLE - 1,)),
            dma((N_SAMPLE - 1,)),
            dma((N_SAMPLE - 1,)),
            dma((N_SAMPLE - 1,)),
        ],
        compiler_params=pltpu.CompilerParams(
            collective_id=0, has_side_effects=True, vmem_limit_bytes=60 * 1024 * 1024
        ),
        name="eqtl",
    )(signature.reshape(1, -1), profile.T, expression, dosage)
    return inter, props_t.T


def solution(mesh):
    placed = (P("sample", "gene"), P("gene", None), P("sample", "variant"), P())
    return jax.shard_map(
        local,
        mesh=mesh,
        in_specs=placed,
        out_specs=(P(("variant", "sample"), "gene"), P("sample", None)),
        check_vma=False,
    )
```

```python
import functools
import math

import jax
import jax.numpy as jnp
from jax import lax
from jax.experimental import pallas as pl
from jax.experimental.pallas import tpu as pltpu
from jax.sharding import PartitionSpec as P

MESH = pl.DeviceIdType.MESH
HIGH = lax.Precision.HIGHEST
F32, BF16 = jnp.float32, jnp.bfloat16
NT = (((1,), (1,)), ((), ()))
N_GENE = 4
N_SAMPLE = 16
N_CHUNK = 4
VMEM_BYTES = 62_000_000
PARTS = ((0, 2), (2, 4), (4, 7))
ORDERS = ("abz", "zab", "bza")


def ldl(gram):
    row = lax.broadcasted_iota(jnp.int32, (8, 8), 0)
    col = lax.broadcasted_iota(jnp.int32, (8, 8), 1)
    eye = (row == col).astype(F32)
    a = jnp.where((row == 7) | (col == 7), eye, gram)
    inv, inv_t = eye, eye
    for j in range(6):
        piv = a[j : j + 1, j : j + 1]
        f_col = jnp.where(row[:, :1] > j, a[:, j : j + 1] / piv, 0.0)
        f_row = jnp.where(col[:1, :] > j, a[j : j + 1, :] / piv, 0.0)
        inv = inv - f_col * inv[j : j + 1, :]
        inv_t = inv_t - inv_t[:, j : j + 1] * f_row
        a = a - f_col * a[j : j + 1, :]
    diag = jnp.sum(a * eye, axis=1, keepdims=True)
    return inv, inv_t, diag


def solve(factor, rhs):
    inv, inv_t, diag = factor
    mid = inv[:, 0:1] * rhs[0:1, :]
    for j in range(1, 7):
        mid = mid + inv[:, j : j + 1] * rhs[j : j + 1, :]
    mid = mid / diag
    out = inv_t[:, 0:1] * mid[0:1, :]
    for j in range(1, 7):
        out = out + inv_t[:, j : j + 1] * mid[j : j + 1, :]
    return out


def kernel(
    scale,
    sig_ref, prof_ref, expr_hbm, dos_hbm,
    inter_ref, props_ref,
    e_v, d_v, d_t, des, sig_sc, m_sc, acc, rc, r1, r2, r3,
    pbuf, rsnd, rrcv, gsnd, grcv, corr_sc, pp_sc, py_sc, fac_sc, tsrc, trcv, tbuf, mix,
    e_sem, d_sem, g_s, g_r, x_s, x_r, p_s, p_r, c_s, c_r, h_s, h_r, t_s, t_r, u_s, u_r,
):
    s_dev, g_dev = e_v.shape
    quarter = s_dev // N_GENE
    half = quarter // 2
    n_cols = g_dev // N_CHUNK
    n_tiles = g_dev // 128
    per_chunk = n_cols // 128
    types = 7
    g = lax.axis_index("gene")
    s = lax.axis_index("sample")
    y, z, c = s // 4, (s // 2) % 2, s % 2
    b = y // 2
    a = (y + b) % 2
    place = {"a": a, "b": b, "z": z}
    other = {
        "a": (2 * b + (1 - a + b) % 2) * 4 + z * 2 + c,
        "b": (2 * (1 - b) + (a + 1 - b) % 2) * 4 + z * 2 + c,
        "z": s + 2 - 4 * z,
    }
    core = s + 1 - 2 * c

    def gene_of(d):
        return {"gene": (g + d) % N_GENE}

    def sample_of(d):
        return {"sample": (s + d) % N_SAMPLE}

    def rows_of(d, h):
        return pl.ds(pl.multiple_of(((g + d) % N_GENE) * quarter + h * half, half), half)

    def load(d, h):
        return pltpu.make_async_copy(expr_hbm.at[rows_of(d, h), :], e_v.at[rows_of(d, h), :], e_sem.at[d, h])

    def remote(src, dst, send, recv, device):
        return pltpu.make_async_remote_copy(
            src_ref=src, dst_ref=dst, send_sem=send, recv_sem=recv, device_id=device, device_id_type=MESH
        )

    for d in (3, 2, 1, 0):
        for h in range(2):
            load(d, h).start()
    dos_copy = pltpu.make_async_copy(dos_hbm, d_v, d_sem)
    dos_copy.start()

    barrier = pltpu.get_barrier_semaphore()
    for d in range(1, N_GENE):
        pl.semaphore_signal(barrier, inc=1, device_id=gene_of(d), device_id_type=MESH)
    for d in range(1, N_SAMPLE):
        pl.semaphore_signal(barrier, inc=1, device_id=sample_of(d), device_id_type=MESH)

    n_sig = sig_ref.shape[1]
    sig_sc[...] = jnp.full(sig_sc.shape, -1, jnp.int32)
    sig_sc[0:1, 0:n_sig] = sig_ref[...]
    cols = []
    for t in range(sig_sc.shape[1] // 128):
        line = sig_sc[0:1, 128 * t : 128 * t + 128].astype(F32)
        cols.append(jnp.transpose(jnp.broadcast_to(line, (128, 128))))
    lane = lax.broadcasted_iota(jnp.int32, (128, 128), 1) + g * g_dev
    m_sc[...] = jnp.zeros(m_sc.shape, F32)
    for t in range(n_tiles):
        ids = (lane + 128 * t).astype(F32)
        hit = jnp.zeros((128, 128), F32)
        for column in cols:
            hit = jnp.where(column == ids, 1.0, hit)
        member = jnp.max(hit, axis=0, keepdims=True)
        m_sc[0:types, 128 * t : 128 * t + 128] = prof_ref[:, 128 * t : 128 * t + 128] * member
    masked = m_sc[...]
    gsnd[...] = jnp.zeros(gsnd.shape, F32)
    gsnd[:, 0:8] = lax.dot_general(masked, masked, NT, precision=HIGH, preferred_element_type=F32)
    top = masked.astype(BF16).astype(F32)
    rest = masked - top
    mid = rest.astype(BF16).astype(F32)
    m3 = jnp.concatenate([top, mid, rest - mid], axis=0).astype(BF16)

    def gram_copy(d):
        return remote(gsnd, grcv.at[d - 1], g_s.at[d - 1], g_r.at[d - 1], gene_of(d))

    def rhs_copy(d):
        return remote(rsnd.at[d], rrcv.at[d - 1], x_s.at[d - 1], x_r.at[d - 1], gene_of(d))

    def rhs_half(i, carry):
        d, h = N_GENE - 1 - i // 2, i % 2
        load(d, h).wait()
        part = lax.dot_general(m3, e_v[rows_of(d, h), :], NT, preferred_element_type=F32)
        rsnd[d, :, pl.ds(pl.multiple_of(h * half, half), half)] = part[0:8] + part[8:16] + part[16:24]

        @pl.when(i == 1)
        def _():
            pl.semaphore_wait(barrier, N_GENE - 1 + N_SAMPLE - 1)
            for peer in range(1, N_GENE):
                gram_copy(peer).start()

        @pl.when((h == 1) & (d > 0))
        def _():
            rhs_copy(d).start()

        return carry

    lax.fori_loop(0, 2 * N_GENE, rhs_half, 0)

    dos_copy.wait()
    for i in range(s_dev // 128):
        piece = d_v[128 * i : 128 * i + 128, :].astype(F32).astype(BF16)
        d_t[:, 128 * i : 128 * i + 128] = jnp.transpose(piece)

    def clear(n, carry):
        acc[n] = jnp.zeros(acc.shape[1:], F32)
        return carry

    lax.fori_loop(0, N_CHUNK, clear, 0)
    py_sc[...] = jnp.zeros(py_sc.shape, F32)
    corr_sc[...] = jnp.zeros(corr_sc.shape, F32)
    pp_sc[...] = jnp.zeros(pp_sc.shape, F32)
    gram = gsnd[:, 0:8]
    for d in range(1, N_GENE):
        gram_copy(d).wait_recv()
        gram = gram + grcv[d - 1, :, 0:8]
    factor = ldl(gram)
    rhs = rsnd[0]
    for d in (3, 2, 1):
        rhs_copy(d).wait_recv()
        rhs = rhs + rrcv[d - 1]
    pbuf[g] = solve(factor, rhs)

    def props_copy(d):
        return remote(pbuf.at[g], pbuf.at[g], p_s.at[d - 1], p_r.at[d - 1], gene_of(d))

    for d in (2, 1, 3):
        props_copy(d).start()

    def quarter_of(d):
        return (g + N_GENE - d) % N_GENE

    def span_of(d):
        return pl.ds(pl.multiple_of(quarter_of(d) * quarter, quarter), quarter)

    def design(d):
        props = pbuf[quarter_of(d)]
        props_ref[:, span_of(d)] = props[0:types]
        top = props.astype(BF16).astype(F32)
        des[d, 896:912, :] = jnp.concatenate([top, props - top], axis=0).astype(BF16)
        for k in range(types):
            wide = jnp.broadcast_to(top[k : k + 1, :], (16, quarter)).astype(BF16)
            for bb in range(2):
                for aa in range(2):
                    for zz in range(2):
                        source = ((2 * bb + (aa + bb) % 2) * 2 + zz) * 16
                        target = (((bb * 2 + aa) * 2 + zz) * types + k) * 16
                        des[d, target : target + 16, :] = d_t[source : source + 16, span_of(d)] * wide

    def small_term(d):
        props = pbuf[quarter_of(d)]
        top = props.astype(BF16).astype(F32)
        highs, lows = [], []
        for k in range(types):
            weight = jnp.broadcast_to(top[k : k + 1, :], (8, quarter)) * props
            high = weight.astype(BF16).astype(F32)
            highs.append(high)
            lows.append(weight - high)
        w = jnp.concatenate(highs + lows, axis=0).astype(BF16)
        corr = lax.dot_general(d_t[:, span_of(d)], w, NT, preferred_element_type=F32)
        both = des[d, 896:912, :]
        pp = lax.dot_general(both, both, NT, preferred_element_type=F32)
        corr_sc[:, 0 : 16 * types] += corr
        pp_sc[:, 0:16] += pp[0:8] + pp[8:16]

    def term(n, d):
        columns = pl.ds(pl.multiple_of(n * n_cols, n_cols), n_cols)
        value = jnp.dot(des[d], e_v[span_of(d), columns], preferred_element_type=F32)
        acc[n] += value[0:896].reshape(acc.shape[1:])
        py_sc[n] += value[896:904] + value[904:912]

    def core_copy(n):
        return remote(acc.at[n, :, :, :, :, 1 - c], rc.at[n], c_s.at[n], c_r.at[n], {"sample": core})

    def halving(n, part, step):
        axes = ORDERS[(part + n) % 3]
        ks = slice(*PARTS[part])
        kept = {axis: place[axis] for axis in axes[:step]}
        axis = axes[step]

        def block(fixed):
            return (n,) + tuple(fixed.get(name, slice(None)) for name in "baz") + (ks, c)

        landing = ((r1, r2, r3)[step])[part].at[n]
        copy = remote(
            acc.at[block({**kept, axis: 1 - place[axis]})],
            landing,
            h_s.at[n, part, step],
            h_r.at[n, part, step],
            {"sample": other[axis]},
        )
        return copy, block({**kept, axis: place[axis]}), landing

    def across(n):
        core_copy(n).wait_recv()
        acc[n, :, :, :, :, c] += rc[n]
        for part in range(3):
            halving(n, part, 0)[0].start()

    def onward(n, step):
        for part in range(3):
            copy, kept, landing = halving(n, part, step)
            copy.wait_recv()
            acc[kept] += landing[...]
            halving(n, part, step + 1)[0].start()

    def tile_copy(d):
        return remote(tsrc.at[(s + d) % N_SAMPLE], trcv.at[d - 1], t_s.at[d - 1], t_r.at[d - 1], sample_of(d))

    def spread_copy(d):
        return remote(tbuf.at[s], tbuf.at[s], u_s.at[d - 1], u_r.at[d - 1], sample_of(d))

    def start_tiles(d, carry):
        tile_copy(d).start()
        return carry

    def take_tile(d, carry):
        tile_copy(d).wait_recv()
        return carry + trcv[d - 1]

    def start_spread(d, carry):
        spread_copy(d).start()
        return carry

    def take_spread(d, carry):
        spread_copy(d).wait_recv()
        return carry

    spot = lax.broadcasted_iota(jnp.int32, (8, 128), 1)
    n_kj = 8 * types

    def send_tiles():
        pp = pp_sc[...]
        pp = pltpu.roll(pp + pltpu.roll(pp, 120, 1), n_kj, 1)
        for i in range(N_SAMPLE):
            corr = corr_sc[8 * i : 8 * i + 8, :]
            corr = corr + pltpu.roll(corr, 128 - n_kj, 1)
            at = 64 * i
            py = py_sc[at // n_cols, :, at % n_cols // 128 * 128 : at % n_cols // 128 * 128 + 128]
            if i % 2 == 0:
                py = pltpu.roll(py, 64, 1)
            tsrc[i] = jnp.where(spot < n_kj, corr, jnp.where(spot < 64, pp, py))
        lax.fori_loop(1, N_SAMPLE, start_tiles, 0)

    def spread_tiles():
        total = lax.fori_loop(1, N_SAMPLE, take_tile, tsrc[s])
        tbuf[s] = total
        lax.fori_loop(1, N_SAMPLE, start_spread, 0)
        corr_sc[0:8, :] = total
        inv, inv_t, diag = ldl(pltpu.roll(total, 128 - n_kj, 1)[:, 0:8])
        fac_sc[0, :, 0:8] = inv
        fac_sc[1, :, 0:8] = inv_t
        fac_sc[2, :, 0:1] = diag

    def solve_coef():
        lax.fori_loop(1, N_SAMPLE, take_spread, 0)
        factor = fac_sc[0, :, 0:8], fac_sc[1, :, 0:8], fac_sc[2, :, 0:1]
        tiles = [jnp.where(spot < 64, pltpu.roll(tbuf[2 * i], 64, 1), tbuf[2 * i + 1]) for i in range(n_tiles)]
        m_sc[...] = solve(factor, jnp.concatenate(tiles, axis=1))

    def finish(n):
        corr = corr_sc[0:8, :]
        coef = m_sc[:, n * n_cols : (n + 1) * n_cols]
        for part in range(3):
            copy, kept, landing = halving(n, part, 2)
            copy.wait_recv()
            value = acc[kept] + landing[...]
            for k in range(*PARTS[part]):
                out = value[k - PARTS[part][0]]
                for j in range(types):
                    out = out - corr[:, 8 * k + j : 8 * k + j + 1] * coef[j : j + 1, :]
                out = out * scale
                for i in range(per_chunk):
                    mix[n * per_chunk + i, pl.ds(k, 8, stride=types), :] = out[:, 128 * i : 128 * i + 128]
        for i in range(n * per_chunk, (n + 1) * per_chunk):
            inter_ref[:, 128 * i : 128 * i + 128] = mix[i]

    design(0)

    def step(e, carry):
        rest = (e + 12) // 16
        n = (1 - rest) * e + rest * ((e - 4) // 3)
        t = rest * (1 + (e - 4) % 3)

        @pl.when(e == 4)
        def _():
            for d in (1, 3, 2):
                props_copy(d).wait_recv()
                design(d)

        term(n, t)

        for chunk in range(N_CHUNK):
            @pl.when(e == 3 * chunk + 6)
            def _(chunk=chunk):
                core_copy(chunk).start()

        @pl.when(e == 3)
        def _():
            small_term(0)

        for chunk in range(N_CHUNK - 1):
            @pl.when(e == 3 * chunk + 8)
            def _(chunk=chunk):
                across(chunk)

        @pl.when(e == 14)
        def _():
            onward(0, 0)

        return carry

    lax.fori_loop(0, 4 * N_CHUNK, step, 0)

    def small_more(d, carry):
        small_term(d)
        return carry

    lax.fori_loop(1, N_GENE, small_more, 0)
    across(3)
    onward(1, 0)
    send_tiles()
    onward(0, 1)
    onward(2, 0)
    onward(1, 1)
    spread_tiles()
    onward(3, 0)
    onward(2, 1)
    onward(3, 1)
    solve_coef()
    for n in range(N_CHUNK):
        finish(n)

    for d in range(1, N_GENE):
        gram_copy(d).wait_send()
        rhs_copy(d).wait_send()
        props_copy(d).wait_send()
    for n in range(N_CHUNK):
        core_copy(n).wait_send()
        for part in range(3):
            for step in range(3):
                halving(n, part, step)[0].wait_send()

    def drain_tiles(d, carry):
        tile_copy(d).wait_send()
        spread_copy(d).wait_send()
        return carry

    lax.fori_loop(1, N_SAMPLE, drain_tiles, 0)


def local(expression, profile, dosage, signature):
    s_dev, g_dev = expression.shape
    v_dev = dosage.shape[1]
    types = profile.shape[1]
    quarter, n_cols = s_dev // N_GENE, g_dev // N_CHUNK
    scale = 1.0 / math.sqrt(s_dev * N_SAMPLE)
    sig_cols = -(-signature.shape[0] // 128) * 128
    sizes = [hi - lo for lo, hi in PARTS]
    vmem, dma = pltpu.VMEM, pltpu.SemaphoreType.DMA
    inter, props_t = pl.pallas_call(
        functools.partial(kernel, scale),
        out_shape=(
            vmem((v_dev * types // N_SAMPLE, g_dev), F32),
            vmem((types, s_dev), F32),
        ),
        in_specs=[
            pl.BlockSpec(memory_space=pltpu.VMEM),
            pl.BlockSpec(memory_space=pltpu.VMEM),
            pl.BlockSpec(memory_space=pl.ANY),
            pl.BlockSpec(memory_space=pl.ANY),
        ],
        out_specs=(pl.BlockSpec(memory_space=pltpu.VMEM), pl.BlockSpec(memory_space=pltpu.VMEM)),
        scratch_shapes=[
            vmem((s_dev, g_dev), BF16),
            vmem((s_dev, v_dev), jnp.int32),
            vmem((v_dev, s_dev), BF16),
            vmem((N_GENE, v_dev * types + 16, quarter), BF16),
            vmem((1, sig_cols), jnp.int32),
            vmem((8, g_dev), F32),
            vmem((N_CHUNK, 2, 2, 2, types, 2, 8, n_cols), F32),
            vmem((N_CHUNK, 2, 2, 2, types, 8, n_cols), F32),
            [vmem((N_CHUNK, 2, 2, k, 8, n_cols), F32) for k in sizes],
            [vmem((N_CHUNK, 2, k, 8, n_cols), F32) for k in sizes],
            [vmem((N_CHUNK, k, 8, n_cols), F32) for k in sizes],
            vmem((N_GENE, 8, quarter), F32),
            vmem((N_GENE, 8, quarter), F32),
            vmem((N_GENE - 1, 8, quarter), F32),
            vmem((8, 128), F32),
            vmem((N_GENE - 1, 8, 128), F32),
            vmem((v_dev, 128), F32),
            vmem((8, 128), F32),
            vmem((N_CHUNK, 8, n_cols), F32),
            vmem((3, 8, 128), F32),
            vmem((N_SAMPLE, 8, 128), F32),
            vmem((N_SAMPLE - 1, 8, 128), F32),
            vmem((N_SAMPLE, 8, 128), F32),
            vmem((g_dev // 128, 8 * types, 128), F32),
            dma((N_GENE, 2)),
            dma,
            dma((N_GENE - 1,)),
            dma((N_GENE - 1,)),
            dma((N_GENE - 1,)),
            dma((N_GENE - 1,)),
            dma((N_GENE - 1,)),
            dma((N_GENE - 1,)),
            dma((N_CHUNK,)),
            dma((N_CHUNK,)),
            dma((N_CHUNK, 3, 3)),
            dma((N_CHUNK, 3, 3)),
            dma((N_SAMPLE - 1,)),
            dma((N_SAMPLE - 1,)),
            dma((N_SAMPLE - 1,)),
            dma((N_SAMPLE - 1,)),
        ],
        compiler_params=pltpu.CompilerParams(
            collective_id=0, has_side_effects=True, vmem_limit_bytes=VMEM_BYTES
        ),
        name="eqtl",
    )(signature.reshape(1, -1), profile.T, expression, dosage)
    return inter, props_t.T


def solution(mesh):
    placed = (P("sample", "gene"), P("gene", None), P("sample", "variant"), P())
    return jax.shard_map(
        local,
        mesh=mesh,
        in_specs=placed,
        out_specs=(P(("variant", "sample"), "gene"), P("sample", None)),
        check_vma=False,
    )
```

```python
import functools
import math

import jax
import jax.numpy as jnp
from jax import lax
from jax.experimental import pallas as pl
from jax.experimental.pallas import tpu as pltpu
from jax.sharding import PartitionSpec as P

MESH = pl.DeviceIdType.MESH
HIGH = lax.Precision.HIGHEST
F32, BF16 = jnp.float32, jnp.bfloat16
NT = (((1,), (1,)), ((), ()))
N_GENE = 4
N_SAMPLE = 16
N_CHUNK = 4
VMEM_BYTES = 62_000_000
PARTS = ((0, 2), (2, 4), (4, 7))
ORDERS = ("abz", "zab", "bza")


def ldl(gram):
    row = lax.broadcasted_iota(jnp.int32, (8, 8), 0)
    col = lax.broadcasted_iota(jnp.int32, (8, 8), 1)
    eye = (row == col).astype(F32)
    a = jnp.where((row == 7) | (col == 7), eye, gram)
    inv, inv_t = eye, eye
    for j in range(6):
        piv = a[j : j + 1, j : j + 1]
        f_col = jnp.where(row[:, :1] > j, a[:, j : j + 1] / piv, 0.0)
        f_row = jnp.where(col[:1, :] > j, a[j : j + 1, :] / piv, 0.0)
        inv = inv - f_col * inv[j : j + 1, :]
        inv_t = inv_t - inv_t[:, j : j + 1] * f_row
        a = a - f_col * a[j : j + 1, :]
    diag = jnp.sum(a * eye, axis=1, keepdims=True)
    return inv, inv_t, diag


def solve(factor, rhs):
    inv, inv_t, diag = factor
    mid = inv[:, 0:1] * rhs[0:1, :]
    for j in range(1, 7):
        mid = mid + inv[:, j : j + 1] * rhs[j : j + 1, :]
    mid = mid / diag
    out = inv_t[:, 0:1] * mid[0:1, :]
    for j in range(1, 7):
        out = out + inv_t[:, j : j + 1] * mid[j : j + 1, :]
    return out


def kernel(
    scale,
    sig_hbm, prof_hbm, expr_hbm, dos_hbm,
    inter_ref, props_ref,
    e_v, d_v, d_t, des, sig_ref, prof_ref, sig_sc, m_sc, acc, rc, r1, r2, r3,
    pbuf, rsnd, rrcv, gsnd, grcv, corr_sc, pp_sc, py_sc, fac_sc, tsrc, trcv, tbuf, mix,
    e_sem, d_sem, i_sem, g_s, g_r, x_s, x_r, p_s, p_r, c_s, c_r, h_s, h_r, t_s, t_r, u_s, u_r,
):
    s_dev, g_dev = e_v.shape
    quarter = s_dev // N_GENE
    half = quarter // 2
    n_cols = g_dev // N_CHUNK
    n_tiles = g_dev // 128
    per_chunk = n_cols // 128
    types = 7
    g = lax.axis_index("gene")
    s = lax.axis_index("sample")
    y, z, c = s // 4, (s // 2) % 2, s % 2
    b = y // 2
    a = (y + b) % 2
    place = {"a": a, "b": b, "z": z}
    other = {
        "a": (2 * b + (1 - a + b) % 2) * 4 + z * 2 + c,
        "b": (2 * (1 - b) + (a + 1 - b) % 2) * 4 + z * 2 + c,
        "z": s + 2 - 4 * z,
    }
    core = s + 1 - 2 * c

    def gene_of(d):
        return {"gene": (g + d) % N_GENE}

    def sample_of(d):
        return {"sample": (s + d) % N_SAMPLE}

    def quarter_of(d):
        return (g + N_GENE - d) % N_GENE

    def load(d, h):
        source = pl.ds(pl.multiple_of(quarter_of(d) * quarter + h * half, half), half)
        target = pl.ds(pl.multiple_of(d * quarter + h * half, half), half)
        return pltpu.make_async_copy(expr_hbm.at[source, :], e_v.at[target, :], e_sem.at[d, h])

    def load_dosage(d):
        source = pl.ds(pl.multiple_of(quarter_of(d) * quarter, quarter), quarter)
        return pltpu.make_async_copy(dos_hbm.at[source, :], d_v.at[pl.ds(d * quarter, quarter), :], d_sem.at[d])

    def remote(src, dst, send, recv, device):
        return pltpu.make_async_remote_copy(
            src_ref=src, dst_ref=dst, send_sem=send, recv_sem=recv, device_id=device, device_id_type=MESH
        )

    sig_copy = pltpu.make_async_copy(sig_hbm, sig_ref, i_sem.at[0])
    prof_copy = pltpu.make_async_copy(prof_hbm, prof_ref, i_sem.at[1])
    sig_copy.start()
    prof_copy.start()
    for d in (1, 2, 3, 0):
        for h in range(2):
            load(d, h).start()
    for d in range(N_GENE):
        load_dosage(d).start()

    barrier = pltpu.get_barrier_semaphore()
    for d in range(1, N_GENE):
        pl.semaphore_signal(barrier, inc=1, device_id=gene_of(d), device_id_type=MESH)
    for d in range(1, N_SAMPLE):
        pl.semaphore_signal(barrier, inc=1, device_id=sample_of(d), device_id_type=MESH)

    n_sig = sig_ref.shape[1]
    sig_sc[...] = jnp.full(sig_sc.shape, -1, jnp.int32)
    sig_copy.wait()
    sig_sc[0:1, 0:n_sig] = sig_ref[...]
    cols = []
    for t in range(sig_sc.shape[1] // 128):
        line = sig_sc[0:1, 128 * t : 128 * t + 128].astype(F32)
        cols.append(jnp.transpose(jnp.broadcast_to(line, (128, 128))))
    lane = lax.broadcasted_iota(jnp.int32, (128, 128), 1) + g * g_dev
    m_sc[...] = jnp.zeros(m_sc.shape, F32)
    prof_copy.wait()
    for t in range(n_tiles):
        ids = (lane + 128 * t).astype(F32)
        hit = jnp.zeros((128, 128), F32)
        for column in cols:
            hit = jnp.where(column == ids, 1.0, hit)
        member = jnp.max(hit, axis=0, keepdims=True)
        m_sc[0:types, 128 * t : 128 * t + 128] = prof_ref[:, 128 * t : 128 * t + 128] * member
    masked = m_sc[...]
    gsnd[...] = jnp.zeros(gsnd.shape, F32)
    gsnd[:, 0:8] = lax.dot_general(masked, masked, NT, precision=HIGH, preferred_element_type=F32)
    top = masked.astype(BF16).astype(F32)
    rest = masked - top
    mid = rest.astype(BF16).astype(F32)
    m3 = jnp.concatenate([top, mid, rest - mid], axis=0).astype(BF16)

    def gram_copy(d):
        return remote(gsnd, grcv.at[d - 1], g_s.at[d - 1], g_r.at[d - 1], gene_of(d))

    def rhs_copy(d):
        return remote(rsnd.at[d], rrcv.at[d - 1], x_s.at[d - 1], x_r.at[d - 1], gene_of(d))

    def rhs_half(i, carry):
        d, h = N_GENE - 1 - i // 2, i % 2
        at = (N_GENE - d) % N_GENE
        load(at, h).wait()
        rows = pl.ds(pl.multiple_of(at * quarter + h * half, half), half)
        part = lax.dot_general(m3, e_v[rows, :], NT, preferred_element_type=F32)
        rsnd[d, :, pl.ds(pl.multiple_of(h * half, half), half)] = part[0:8] + part[8:16] + part[16:24]

        @pl.when(i == 1)
        def _():
            pl.semaphore_wait(barrier, N_GENE - 1 + N_SAMPLE - 1)
            for peer in range(1, N_GENE):
                gram_copy(peer).start()

        @pl.when((h == 1) & (d > 0))
        def _():
            rhs_copy(d).start()

        return carry

    lax.fori_loop(0, 2 * N_GENE, rhs_half, 0)

    for d in range(N_GENE):
        load_dosage(d).wait()
    for i in range(s_dev // 128):
        piece = d_v[128 * i : 128 * i + 128, :].astype(F32).astype(BF16)
        d_t[:, 128 * i : 128 * i + 128] = jnp.transpose(piece)
    corr_sc[...] = jnp.zeros(corr_sc.shape, F32)
    pp_sc[...] = jnp.zeros(pp_sc.shape, F32)
    gram = gsnd[:, 0:8]
    for d in range(1, N_GENE):
        gram_copy(d).wait_recv()
        gram = gram + grcv[d - 1, :, 0:8]
    factor = ldl(gram)
    rhs = rsnd[0]
    for d in (3, 2, 1):
        rhs_copy(d).wait_recv()
        rhs = rhs + rrcv[d - 1]
    pbuf[g] = solve(factor, rhs)

    def props_copy(d):
        return remote(pbuf.at[g], pbuf.at[g], p_s.at[d - 1], p_r.at[d - 1], gene_of(d))

    for d in (2, 1, 3):
        props_copy(d).start()

    def span_of(d):
        return slice(d * quarter, (d + 1) * quarter)

    def design(d):
        props = pbuf[quarter_of(d)]
        props_ref[:, pl.ds(pl.multiple_of(quarter_of(d) * quarter, quarter), quarter)] = props[0:types]
        top = props.astype(BF16).astype(F32)
        des[896:912, span_of(d)] = jnp.concatenate([top, props - top], axis=0).astype(BF16)
        for k in range(types):
            wide = jnp.broadcast_to(top[k : k + 1, :], (16, quarter)).astype(BF16)
            for bb in range(2):
                for aa in range(2):
                    for zz in range(2):
                        source = ((2 * bb + (aa + bb) % 2) * 2 + zz) * 16
                        target = (((bb * 2 + aa) * 2 + zz) * types + k) * 16
                        des[target : target + 16, span_of(d)] = d_t[source : source + 16, span_of(d)] * wide

    def small_term(d):
        span = pl.ds(pl.multiple_of(d * quarter, quarter), quarter)
        props = pbuf[quarter_of(d)]
        top = props.astype(BF16).astype(F32)
        highs, lows = [], []
        for k in range(types):
            weight = jnp.broadcast_to(top[k : k + 1, :], (8, quarter)) * props
            high = weight.astype(BF16).astype(F32)
            highs.append(high)
            lows.append(weight - high)
        w = jnp.concatenate(highs + lows, axis=0).astype(BF16)
        corr = lax.dot_general(d_t[:, span], w, NT, preferred_element_type=F32)
        both = des[896:912, span]
        pp = lax.dot_general(both, both, NT, preferred_element_type=F32)
        corr_sc[:, 0 : 16 * types] += corr
        pp_sc[:, 0:16] += pp[0:8] + pp[8:16]

    def term(n, first):
        columns = pl.ds(pl.multiple_of(n * n_cols, n_cols), n_cols)
        span = slice(0, quarter) if first else slice(quarter, s_dev)
        value = jnp.dot(des[:, span], e_v[span, columns], preferred_element_type=F32)
        body, tail = value[0:896].reshape(acc.shape[1:]), value[896:904] + value[904:912]
        acc[n] = body if first else acc[n] + body
        py_sc[n] = tail if first else py_sc[n] + tail

    def core_copy(n):
        return remote(acc.at[n, :, :, :, :, 1 - c], rc.at[n], c_s.at[n], c_r.at[n], {"sample": core})

    def halving(n, part, step):
        axes = ORDERS[(part + n) % 3]
        ks = slice(*PARTS[part])
        kept = {axis: place[axis] for axis in axes[:step]}
        axis = axes[step]

        def block(fixed):
            return (n,) + tuple(fixed.get(name, slice(None)) for name in "baz") + (ks, c)

        landing = ((r1, r2, r3)[step])[part].at[n]
        copy = remote(
            acc.at[block({**kept, axis: 1 - place[axis]})],
            landing,
            h_s.at[n, part, step],
            h_r.at[n, part, step],
            {"sample": other[axis]},
        )
        return copy, block({**kept, axis: place[axis]}), landing

    def across(n):
        core_copy(n).wait_recv()
        acc[n, :, :, :, :, c] += rc[n]
        for part in range(3):
            halving(n, part, 0)[0].start()

    def onward(n, step):
        for part in range(3):
            copy, kept, landing = halving(n, part, step)
            copy.wait_recv()
            acc[kept] += landing[...]
            halving(n, part, step + 1)[0].start()

    def tile_copy(d):
        return remote(tsrc.at[(s + d) % N_SAMPLE], trcv.at[d - 1], t_s.at[d - 1], t_r.at[d - 1], sample_of(d))

    def spread_copy(d):
        return remote(tbuf.at[s], tbuf.at[s], u_s.at[d - 1], u_r.at[d - 1], sample_of(d))

    def start_tiles(d, carry):
        tile_copy(d).start()
        return carry

    def take_tile(d, carry):
        tile_copy(d).wait_recv()
        return carry + trcv[d - 1]

    def start_spread(d, carry):
        spread_copy(d).start()
        return carry

    def take_spread(d, carry):
        spread_copy(d).wait_recv()
        return carry

    spot = lax.broadcasted_iota(jnp.int32, (8, 128), 1)
    n_kj = 8 * types

    def send_tiles():
        pp = pp_sc[...]
        pp = pltpu.roll(pp + pltpu.roll(pp, 120, 1), n_kj, 1)
        for i in range(N_SAMPLE):
            corr = corr_sc[8 * i : 8 * i + 8, :]
            corr = corr + pltpu.roll(corr, 128 - n_kj, 1)
            at = 64 * i
            py = py_sc[at // n_cols, :, at % n_cols // 128 * 128 : at % n_cols // 128 * 128 + 128]
            if i % 2 == 0:
                py = pltpu.roll(py, 64, 1)
            tsrc[i] = jnp.where(spot < n_kj, corr, jnp.where(spot < 64, pp, py))
        lax.fori_loop(1, N_SAMPLE, start_tiles, 0)

    def spread_tiles():
        total = lax.fori_loop(1, N_SAMPLE, take_tile, tsrc[s])
        tbuf[s] = total
        lax.fori_loop(1, N_SAMPLE, start_spread, 0)
        corr_sc[0:8, :] = total
        inv, inv_t, diag = ldl(pltpu.roll(total, 128 - n_kj, 1)[:, 0:8])
        fac_sc[0, :, 0:8] = inv
        fac_sc[1, :, 0:8] = inv_t
        fac_sc[2, :, 0:1] = diag

    def solve_coef():
        lax.fori_loop(1, N_SAMPLE, take_spread, 0)
        factor = fac_sc[0, :, 0:8], fac_sc[1, :, 0:8], fac_sc[2, :, 0:1]
        tiles = [jnp.where(spot < 64, pltpu.roll(tbuf[2 * i], 64, 1), tbuf[2 * i + 1]) for i in range(n_tiles)]
        m_sc[...] = solve(factor, jnp.concatenate(tiles, axis=1))

    def finish(n):
        corr = corr_sc[0:8, :]
        coef = m_sc[:, n * n_cols : (n + 1) * n_cols]
        for part in range(3):
            copy, kept, landing = halving(n, part, 2)
            copy.wait_recv()
            value = acc[kept] + landing[...]
            for k in range(*PARTS[part]):
                out = value[k - PARTS[part][0]]
                for j in range(types):
                    out = out - corr[:, 8 * k + j : 8 * k + j + 1] * coef[j : j + 1, :]
                out = out * scale
                for i in range(per_chunk):
                    mix[n * per_chunk + i, pl.ds(k, 8, stride=types), :] = out[:, 128 * i : 128 * i + 128]
        for i in range(n * per_chunk, (n + 1) * per_chunk):
            inter_ref[:, 128 * i : 128 * i + 128] = mix[i]

    design(0)

    def own(n, carry):
        term(n, True)
        return carry

    lax.fori_loop(0, N_CHUNK, own, 0)
    small_term(0)
    for d in (1, 3, 2):
        props_copy(d).wait_recv()
        design(d)

    def others(n, carry):
        term(n, False)
        core_copy(n).start()
        for chunk in range(1, N_CHUNK):
            @pl.when(n == chunk)
            def _(chunk=chunk):
                across(chunk - 1)

        return carry

    lax.fori_loop(0, N_CHUNK, others, 0)

    def small_more(d, carry):
        small_term(d)
        return carry

    lax.fori_loop(1, N_GENE, small_more, 0)
    onward(0, 0)
    across(3)
    send_tiles()
    onward(1, 0)
    onward(0, 1)
    onward(2, 0)
    onward(3, 0)
    spread_tiles()
    onward(1, 1)
    onward(2, 1)
    onward(3, 1)
    solve_coef()
    for n in range(N_CHUNK):
        finish(n)

    for d in range(1, N_GENE):
        gram_copy(d).wait_send()
        rhs_copy(d).wait_send()
        props_copy(d).wait_send()
    for n in range(N_CHUNK):
        core_copy(n).wait_send()
        for part in range(3):
            for step in range(3):
                halving(n, part, step)[0].wait_send()

    def drain_tiles(d, carry):
        tile_copy(d).wait_send()
        spread_copy(d).wait_send()
        return carry

    lax.fori_loop(1, N_SAMPLE, drain_tiles, 0)


def local(expression, profile, dosage, signature):
    s_dev, g_dev = expression.shape
    v_dev = dosage.shape[1]
    types = profile.shape[1]
    quarter, n_cols = s_dev // N_GENE, g_dev // N_CHUNK
    scale = 1.0 / math.sqrt(s_dev * N_SAMPLE)
    sig_cols = -(-signature.shape[0] // 128) * 128
    sizes = [hi - lo for lo, hi in PARTS]
    vmem, dma = pltpu.VMEM, pltpu.SemaphoreType.DMA
    inter, props_t = pl.pallas_call(
        functools.partial(kernel, scale),
        out_shape=(
            vmem((v_dev * types // N_SAMPLE, g_dev), F32),
            vmem((types, s_dev), F32),
        ),
        in_specs=[
            pl.BlockSpec(memory_space=pl.ANY),
            pl.BlockSpec(memory_space=pl.ANY),
            pl.BlockSpec(memory_space=pl.ANY),
            pl.BlockSpec(memory_space=pl.ANY),
        ],
        out_specs=(pl.BlockSpec(memory_space=pltpu.VMEM), pl.BlockSpec(memory_space=pltpu.VMEM)),
        scratch_shapes=[
            vmem((s_dev, g_dev), BF16),
            vmem((s_dev, v_dev), jnp.int32),
            vmem((v_dev, s_dev), BF16),
            vmem((v_dev * types + 16, s_dev), BF16),
            vmem((1, signature.shape[0]), jnp.int32),
            vmem((types, g_dev), F32),
            vmem((1, sig_cols), jnp.int32),
            vmem((8, g_dev), F32),
            vmem((N_CHUNK, 2, 2, 2, types, 2, 8, n_cols), F32),
            vmem((N_CHUNK, 2, 2, 2, types, 8, n_cols), F32),
            [vmem((N_CHUNK, 2, 2, k, 8, n_cols), F32) for k in sizes],
            [vmem((N_CHUNK, 2, k, 8, n_cols), F32) for k in sizes],
            [vmem((N_CHUNK, k, 8, n_cols), F32) for k in sizes],
            vmem((N_GENE, 8, quarter), F32),
            vmem((N_GENE, 8, quarter), F32),
            vmem((N_GENE - 1, 8, quarter), F32),
            vmem((8, 128), F32),
            vmem((N_GENE - 1, 8, 128), F32),
            vmem((v_dev, 128), F32),
            vmem((8, 128), F32),
            vmem((N_CHUNK, 8, n_cols), F32),
            vmem((3, 8, 128), F32),
            vmem((N_SAMPLE, 8, 128), F32),
            vmem((N_SAMPLE - 1, 8, 128), F32),
            vmem((N_SAMPLE, 8, 128), F32),
            vmem((g_dev // 128, 8 * types, 128), F32),
            dma((N_GENE, 2)),
            dma((N_GENE,)),
            dma((2,)),
            dma((N_GENE - 1,)),
            dma((N_GENE - 1,)),
            dma((N_GENE - 1,)),
            dma((N_GENE - 1,)),
            dma((N_GENE - 1,)),
            dma((N_GENE - 1,)),
            dma((N_CHUNK,)),
            dma((N_CHUNK,)),
            dma((N_CHUNK, 3, 3)),
            dma((N_CHUNK, 3, 3)),
            dma((N_SAMPLE - 1,)),
            dma((N_SAMPLE - 1,)),
            dma((N_SAMPLE - 1,)),
            dma((N_SAMPLE - 1,)),
        ],
        compiler_params=pltpu.CompilerParams(
            collective_id=0, has_side_effects=True, vmem_limit_bytes=VMEM_BYTES
        ),
        name="eqtl",
    )(signature.reshape(1, -1), profile.T, expression, dosage)
    return inter, props_t.T


def solution(mesh):
    placed = (P("sample", "gene"), P("gene", None), P("sample", "variant"), P())
    return jax.shard_map(
        local,
        mesh=mesh,
        in_specs=placed,
        out_specs=(P(("variant", "sample"), "gene"), P("sample", None)),
        check_vma=False,
    )
```

```python
import functools
import math

import jax
import jax.numpy as jnp
from jax import lax
from jax.experimental import pallas as pl
from jax.experimental.pallas import tpu as pltpu
from jax.sharding import PartitionSpec as P

MESH = pl.DeviceIdType.MESH
HIGH = lax.Precision.HIGHEST
F32, BF16 = jnp.float32, jnp.bfloat16
NT = (((1,), (1,)), ((), ()))
N_GENE = 4
N_SAMPLE = 16
N_CHUNK = 4
VMEM_BYTES = 62_000_000
PARTS = ((0, 2), (2, 4), (4, 7))
ORDERS = ("abz", "zab", "bza")


def ldl(gram):
    row = lax.broadcasted_iota(jnp.int32, (8, 8), 0)
    col = lax.broadcasted_iota(jnp.int32, (8, 8), 1)
    eye = (row == col).astype(F32)
    a = jnp.where((row == 7) | (col == 7), eye, gram)
    inv, inv_t = eye, eye
    for j in range(6):
        piv = a[j : j + 1, j : j + 1]
        f_col = jnp.where(row[:, :1] > j, a[:, j : j + 1] / piv, 0.0)
        f_row = jnp.where(col[:1, :] > j, a[j : j + 1, :] / piv, 0.0)
        inv = inv - f_col * inv[j : j + 1, :]
        inv_t = inv_t - inv_t[:, j : j + 1] * f_row
        a = a - f_col * a[j : j + 1, :]
    diag = jnp.sum(a * eye, axis=1, keepdims=True)
    return inv, inv_t, diag


def solve(factor, rhs):
    inv, inv_t, diag = factor
    mid = inv[:, 0:1] * rhs[0:1, :]
    for j in range(1, 7):
        mid = mid + inv[:, j : j + 1] * rhs[j : j + 1, :]
    mid = mid / diag
    out = inv_t[:, 0:1] * mid[0:1, :]
    for j in range(1, 7):
        out = out + inv_t[:, j : j + 1] * mid[j : j + 1, :]
    return out


def kernel(
    scale,
    sig_hbm, prof_hbm, expr_hbm, dos_hbm,
    inter_ref, props_ref,
    e_v, d_v, d_t, des, sig_ref, prof_ref, sig_sc, m_sc, acc, rc, r1, r2, r3,
    pbuf, rsnd, rrcv, gsnd, grcv, corr_sc, pp_sc, py_sc, fac_sc, tsrc, trcv, tbuf, mix,
    e_sem, d_sem, i_sem, sent, g_r, x_r, p_r, c_r, h_r, t_r, u_r,
):
    s_dev, g_dev = e_v.shape
    quarter = s_dev // N_GENE
    half = quarter // 2
    n_cols = g_dev // N_CHUNK
    n_tiles = g_dev // 128
    per_chunk = n_cols // 128
    types = 7
    g = lax.axis_index("gene")
    s = lax.axis_index("sample")
    y, z, c = s // 4, (s // 2) % 2, s % 2
    b = y // 2
    a = (y + b) % 2
    place = {"a": a, "b": b, "z": z}
    other = {
        "a": (2 * b + (1 - a + b) % 2) * 4 + z * 2 + c,
        "b": (2 * (1 - b) + (a + 1 - b) % 2) * 4 + z * 2 + c,
        "z": s + 2 - 4 * z,
    }
    core = s + 1 - 2 * c

    def gene_of(d):
        return {"gene": (g + d) % N_GENE}

    def sample_of(d):
        return {"sample": (s + d) % N_SAMPLE}

    def quarter_of(d):
        return (g + N_GENE - d) % N_GENE

    def load(d, h):
        source = pl.ds(pl.multiple_of(quarter_of(d) * quarter + h * half, half), half)
        target = pl.ds(pl.multiple_of(d * quarter + h * half, half), half)
        return pltpu.make_async_copy(expr_hbm.at[source, :], e_v.at[target, :], e_sem.at[d, h])

    def load_dosage(d):
        source = pl.ds(pl.multiple_of(quarter_of(d) * quarter, quarter), quarter)
        return pltpu.make_async_copy(dos_hbm.at[source, :], d_v.at[pl.ds(d * quarter, quarter), :], d_sem.at[d])

    def remote(src, dst, recv, device):
        return pltpu.make_async_remote_copy(
            src_ref=src, dst_ref=dst, send_sem=sent, recv_sem=recv, device_id=device, device_id_type=MESH
        )

    sig_copy = pltpu.make_async_copy(sig_hbm, sig_ref, i_sem.at[0])
    prof_copy = pltpu.make_async_copy(prof_hbm, prof_ref, i_sem.at[1])
    sig_copy.start()
    prof_copy.start()
    for h in range(2):
        load(1, h).start()

    barrier = pltpu.get_barrier_semaphore()
    for d in range(1, N_GENE):
        pl.semaphore_signal(barrier, inc=1, device_id=gene_of(d), device_id_type=MESH)
    for d in range(1, N_SAMPLE):
        pl.semaphore_signal(barrier, inc=1, device_id=sample_of(d), device_id_type=MESH)

    n_sig = sig_ref.shape[1]
    sig_sc[...] = jnp.full(sig_sc.shape, -1, jnp.int32)
    sig_copy.wait()
    prof_copy.wait()
    for d in (2, 3, 0):
        for h in range(2):
            load(d, h).start()
    for d in range(N_GENE):
        load_dosage(d).start()
    sig_sc[0:1, 0:n_sig] = sig_ref[...]
    cols = []
    for t in range(sig_sc.shape[1] // 128):
        line = sig_sc[0:1, 128 * t : 128 * t + 128].astype(F32)
        cols.append(jnp.transpose(jnp.broadcast_to(line, (128, 128))))
    lane = lax.broadcasted_iota(jnp.int32, (128, 128), 1) + g * g_dev
    m_sc[...] = jnp.zeros(m_sc.shape, F32)
    for t in range(n_tiles):
        ids = (lane + 128 * t).astype(F32)
        hit = jnp.zeros((128, 128), F32)
        for column in cols:
            hit = jnp.where(column == ids, 1.0, hit)
        member = jnp.max(hit, axis=0, keepdims=True)
        m_sc[0:types, 128 * t : 128 * t + 128] = prof_ref[:, 128 * t : 128 * t + 128] * member
    masked = m_sc[...]
    gsnd[...] = jnp.zeros(gsnd.shape, F32)
    gsnd[:, 0:8] = lax.dot_general(masked, masked, NT, precision=HIGH, preferred_element_type=F32)
    top = masked.astype(BF16).astype(F32)
    rest = masked - top
    mid = rest.astype(BF16).astype(F32)
    m3 = jnp.concatenate([top, mid, rest - mid], axis=0).astype(BF16)

    def gram_copy(d):
        return remote(gsnd, grcv.at[d - 1], g_r.at[d - 1], gene_of(d))

    def rhs_copy(d):
        return remote(rsnd.at[d], rrcv.at[d - 1], x_r.at[d - 1], gene_of(d))

    def rhs_half(i, carry):
        d, h = N_GENE - 1 - i // 2, i % 2
        at = (N_GENE - d) % N_GENE
        load(at, h).wait()
        rows = pl.ds(pl.multiple_of(at * quarter + h * half, half), half)
        part = lax.dot_general(m3, e_v[rows, :], NT, preferred_element_type=F32)
        rsnd[d, :, pl.ds(pl.multiple_of(h * half, half), half)] = part[0:8] + part[8:16] + part[16:24]

        @pl.when(i == 1)
        def _():
            pl.semaphore_wait(barrier, N_GENE - 1 + N_SAMPLE - 1)
            for peer in range(1, N_GENE):
                gram_copy(peer).start()

        @pl.when((h == 1) & (d > 0))
        def _():
            rhs_copy(d).start()

        return carry

    lax.fori_loop(0, 2 * N_GENE, rhs_half, 0)

    for d in range(N_GENE):
        load_dosage(d).wait()
    for i in range(s_dev // 128):
        piece = d_v[128 * i : 128 * i + 128, :].astype(F32).astype(BF16)
        d_t[:, 128 * i : 128 * i + 128] = jnp.transpose(piece)
    corr_sc[...] = jnp.zeros(corr_sc.shape, F32)
    pp_sc[...] = jnp.zeros(pp_sc.shape, F32)
    gram = gsnd[:, 0:8]
    for d in range(1, N_GENE):
        gram_copy(d).wait_recv()
        gram = gram + grcv[d - 1, :, 0:8]
    factor = ldl(gram)
    rhs = rsnd[0]
    for d in (3, 2, 1):
        rhs_copy(d).wait_recv()
        rhs = rhs + rrcv[d - 1]
    pbuf[g] = solve(factor, rhs)

    def props_copy(d):
        return remote(pbuf.at[g], pbuf.at[g], p_r.at[d - 1], gene_of(d))

    for d in (2, 1, 3):
        props_copy(d).start()

    def span_of(d):
        return slice(d * quarter, (d + 1) * quarter)

    def design(d):
        props = pbuf[quarter_of(d)]
        props_ref[:, pl.ds(pl.multiple_of(quarter_of(d) * quarter, quarter), quarter)] = props[0:types]
        top = props.astype(BF16).astype(F32)
        des[896:912, span_of(d)] = jnp.concatenate([top, props - top], axis=0).astype(BF16)
        for k in range(types):
            wide = jnp.broadcast_to(top[k : k + 1, :], (16, quarter)).astype(BF16)
            for bb in range(2):
                for aa in range(2):
                    for zz in range(2):
                        source = ((2 * bb + (aa + bb) % 2) * 2 + zz) * 16
                        target = (((bb * 2 + aa) * 2 + zz) * types + k) * 16
                        des[target : target + 16, span_of(d)] = d_t[source : source + 16, span_of(d)] * wide

    def small_term(d):
        span = pl.ds(pl.multiple_of(d * quarter, quarter), quarter)
        props = pbuf[quarter_of(d)]
        top = props.astype(BF16).astype(F32)
        highs, lows = [], []
        for k in range(types):
            weight = jnp.broadcast_to(top[k : k + 1, :], (8, quarter)) * props
            high = weight.astype(BF16).astype(F32)
            highs.append(high)
            lows.append(weight - high)
        w = jnp.concatenate(highs + lows, axis=0).astype(BF16)
        corr = lax.dot_general(d_t[:, span], w, NT, preferred_element_type=F32)
        both = des[896:912, span]
        pp = lax.dot_general(both, both, NT, preferred_element_type=F32)
        corr_sc[:, 0 : 16 * types] += corr
        pp_sc[:, 0:16] += pp[0:8] + pp[8:16]

    def term(n, first):
        columns = pl.ds(pl.multiple_of(n * n_cols, n_cols), n_cols)
        span = slice(0, quarter) if first else slice(quarter, s_dev)
        value = jnp.dot(des[:, span], e_v[span, columns], preferred_element_type=F32)
        body, tail = value[0:896].reshape(acc.shape[1:]), value[896:904] + value[904:912]
        acc[n] = body if first else acc[n] + body
        py_sc[n] = tail if first else py_sc[n] + tail

    def core_copy(n):
        return remote(acc.at[n, :, :, :, :, 1 - c], rc.at[n], c_r.at[n], {"sample": core})

    def halving(n, part, step):
        axes = ORDERS[(part + n) % 3]
        ks = slice(*PARTS[part])
        kept = {axis: place[axis] for axis in axes[:step]}
        axis = axes[step]

        def block(fixed):
            return (n,) + tuple(fixed.get(name, slice(None)) for name in "baz") + (ks, c)

        landing = ((r1, r2, r3)[step])[part].at[n]
        copy = remote(
            acc.at[block({**kept, axis: 1 - place[axis]})],
            landing,
            h_r.at[n, part, step],
            {"sample": other[axis]},
        )
        return copy, block({**kept, axis: place[axis]}), landing

    def across(n):
        core_copy(n).wait_recv()
        acc[n, :, :, :, :, c] += rc[n]
        for part in range(3):
            halving(n, part, 0)[0].start()

    def onward(n, step):
        for part in range(3):
            copy, kept, landing = halving(n, part, step)
            copy.wait_recv()
            acc[kept] += landing[...]
            halving(n, part, step + 1)[0].start()

    def tile_copy(d):
        return remote(tsrc.at[(s + d) % N_SAMPLE], trcv.at[d], t_r, sample_of(d))

    def spread_copy(d):
        return remote(tbuf.at[0], tbuf.at[d], u_r, sample_of(d))

    def start_tiles(d, carry):
        tile_copy(d).start()
        return carry

    def wait_tiles(buffer, recv):
        remote(tsrc.at[1:N_SAMPLE], buffer.at[1:N_SAMPLE], recv, sample_of(1)).wait_recv()

    def start_spread(d, carry):
        spread_copy(d).start()
        return carry

    spot = lax.broadcasted_iota(jnp.int32, (8, 128), 1)
    n_kj = 8 * types

    def send_tiles():
        pp = pp_sc[...]
        pp = pltpu.roll(pp + pltpu.roll(pp, 120, 1), n_kj, 1)
        for i in range(N_SAMPLE):
            corr = corr_sc[8 * i : 8 * i + 8, :]
            corr = corr + pltpu.roll(corr, 128 - n_kj, 1)
            at = 64 * i
            py = py_sc[at // n_cols, :, at % n_cols // 128 * 128 : at % n_cols // 128 * 128 + 128]
            if i % 2 == 0:
                py = pltpu.roll(py, 64, 1)
            tsrc[i] = jnp.where(spot < n_kj, corr, jnp.where(spot < 64, pp, py))
        lax.fori_loop(1, N_SAMPLE, start_tiles, 0)

    def spread_tiles():
        wait_tiles(trcv, t_r)
        total = tsrc[s]
        for d in range(1, N_SAMPLE):
            total = total + trcv[d]
        tbuf[0] = total
        lax.fori_loop(1, N_SAMPLE, start_spread, 0)
        corr_sc[0:8, :] = total
        inv, inv_t, diag = ldl(pltpu.roll(total, 128 - n_kj, 1)[:, 0:8])
        fac_sc[0, :, 0:8] = inv
        fac_sc[1, :, 0:8] = inv_t
        fac_sc[2, :, 0:1] = diag

    def solve_coef():
        wait_tiles(tbuf, u_r)
        factor = fac_sc[0, :, 0:8], fac_sc[1, :, 0:8], fac_sc[2, :, 0:1]
        own = [tbuf[(s + N_SAMPLE - i) % N_SAMPLE] for i in range(N_SAMPLE)]
        tiles = [jnp.where(spot < 64, pltpu.roll(own[2 * i], 64, 1), own[2 * i + 1]) for i in range(n_tiles)]
        m_sc[...] = solve(factor, jnp.concatenate(tiles, axis=1))

    def finish(n):
        corr = corr_sc[0:8, :]
        coef = m_sc[:, n * n_cols : (n + 1) * n_cols]
        for part in range(3):
            copy, kept, landing = halving(n, part, 2)
            copy.wait_recv()
            value = acc[kept] + landing[...]
            for k in range(*PARTS[part]):
                out = value[k - PARTS[part][0]]
                for j in range(types):
                    out = out - corr[:, 8 * k + j : 8 * k + j + 1] * coef[j : j + 1, :]
                out = out * scale
                for i in range(per_chunk):
                    mix[n * per_chunk + i, pl.ds(k, 8, stride=types), :] = out[:, 128 * i : 128 * i + 128]
        for i in range(n * per_chunk, (n + 1) * per_chunk):
            inter_ref[:, 128 * i : 128 * i + 128] = mix[i]

    design(0)

    def own(n, carry):
        term(n, True)
        return carry

    lax.fori_loop(0, N_CHUNK, own, 0)
    for d in (1, 3, 2):
        props_copy(d).wait_recv()
        design(d)

    def others(n, carry):
        term(n, False)
        small_term(n)
        core_copy(n).start()

        @pl.when(n == N_CHUNK - 1)
        def _():
            send_tiles()

        for chunk in range(1, N_CHUNK):
            @pl.when(n == chunk)
            def _(chunk=chunk):
                across(chunk - 1)

        return carry

    lax.fori_loop(0, N_CHUNK, others, 0)

    onward(0, 0)
    across(3)
    onward(1, 0)
    spread_tiles()
    onward(0, 1)
    onward(2, 0)
    onward(3, 0)
    onward(1, 1)
    onward(2, 1)
    solve_coef()
    finish(0)
    onward(3, 1)
    finish(1)
    finish(2)
    finish(3)

    for d in range(1, N_GENE):
        gram_copy(d).wait_send()
        rhs_copy(d).wait_send()
        props_copy(d).wait_send()
    for n in range(N_CHUNK):
        core_copy(n).wait_send()
        for part in range(3):
            for step in range(3):
                halving(n, part, step)[0].wait_send()

    def drain_tiles(d, carry):
        tile_copy(d).wait_send()
        spread_copy(d).wait_send()
        return carry

    lax.fori_loop(1, N_SAMPLE, drain_tiles, 0)


def local(expression, profile, dosage, signature):
    s_dev, g_dev = expression.shape
    v_dev = dosage.shape[1]
    types = profile.shape[1]
    quarter, n_cols = s_dev // N_GENE, g_dev // N_CHUNK
    scale = 1.0 / math.sqrt(s_dev * N_SAMPLE)
    sig_cols = -(-signature.shape[0] // 128) * 128
    sizes = [hi - lo for lo, hi in PARTS]
    vmem, dma = pltpu.VMEM, pltpu.SemaphoreType.DMA
    inter, props_t = pl.pallas_call(
        functools.partial(kernel, scale),
        out_shape=(
            vmem((v_dev * types // N_SAMPLE, g_dev), F32),
            vmem((types, s_dev), F32),
        ),
        in_specs=[
            pl.BlockSpec(memory_space=pl.ANY),
            pl.BlockSpec(memory_space=pl.ANY),
            pl.BlockSpec(memory_space=pl.ANY),
            pl.BlockSpec(memory_space=pl.ANY),
        ],
        out_specs=(pl.BlockSpec(memory_space=pltpu.VMEM), pl.BlockSpec(memory_space=pltpu.VMEM)),
        scratch_shapes=[
            vmem((s_dev, g_dev), BF16),
            vmem((s_dev, v_dev), jnp.int32),
            vmem((v_dev, s_dev), BF16),
            vmem((v_dev * types + 16, s_dev), BF16),
            vmem((1, signature.shape[0]), jnp.int32),
            vmem((types, g_dev), F32),
            vmem((1, sig_cols), jnp.int32),
            vmem((8, g_dev), F32),
            vmem((N_CHUNK, 2, 2, 2, types, 2, 8, n_cols), F32),
            vmem((N_CHUNK, 2, 2, 2, types, 8, n_cols), F32),
            [vmem((N_CHUNK, 2, 2, k, 8, n_cols), F32) for k in sizes],
            [vmem((N_CHUNK, 2, k, 8, n_cols), F32) for k in sizes],
            [vmem((N_CHUNK, k, 8, n_cols), F32) for k in sizes],
            vmem((N_GENE, 8, quarter), F32),
            vmem((N_GENE, 8, quarter), F32),
            vmem((N_GENE - 1, 8, quarter), F32),
            vmem((8, 128), F32),
            vmem((N_GENE - 1, 8, 128), F32),
            vmem((v_dev, 128), F32),
            vmem((8, 128), F32),
            vmem((N_CHUNK, 8, n_cols), F32),
            vmem((3, 8, 128), F32),
            vmem((N_SAMPLE, 8, 128), F32),
            vmem((N_SAMPLE, 8, 128), F32),
            vmem((N_SAMPLE, 8, 128), F32),
            vmem((g_dev // 128, 8 * types, 128), F32),
            dma((N_GENE, 2)),
            dma((N_GENE,)),
            dma((2,)),
            dma,
            dma((N_GENE - 1,)),
            dma((N_GENE - 1,)),
            dma((N_GENE - 1,)),
            dma((N_CHUNK,)),
            dma((N_CHUNK, 3, 3)),
            dma,
            dma,
        ],
        compiler_params=pltpu.CompilerParams(
            collective_id=0, has_side_effects=True, vmem_limit_bytes=VMEM_BYTES
        ),
        name="eqtl",
    )(signature.reshape(1, -1), profile.T, expression, dosage)
    return inter, props_t.T


def solution(mesh):
    placed = (P("sample", "gene"), P("gene", None), P("sample", "variant"), P())
    return jax.shard_map(
        local,
        mesh=mesh,
        in_specs=placed,
        out_specs=(P(("variant", "sample"), "gene"), P("sample", None)),
        check_vma=False,
    )
```

```python
import functools
import math

import jax
import jax.numpy as jnp
from jax import lax
from jax.experimental import pallas as pl
from jax.experimental.pallas import tpu as pltpu
from jax.sharding import PartitionSpec as P

MESH = pl.DeviceIdType.MESH
HIGH = lax.Precision.HIGHEST
F32, BF16 = jnp.float32, jnp.bfloat16
NT = (((1,), (1,)), ((), ()))
N_GENE = 4
N_SAMPLE = 16
N_CHUNK = 4
VMEM_BYTES = 62_000_000
PARTS = ((0, 2), (2, 4), (4, 7))
ORDERS = (
    ("abz", "zab", "baz"),
    ("azb", "zab", "zab"),
    ("bza", "abz", "abz"),
    ("zba", "zab", "bza"),
)
DURING = {
    (1, 0): ((0, 0, -1),),
    (1, 1): ((0, 1, -1),),
    (1, 2): ((0, 2, -1), (1, 0, -1)),
    (2, 0): ((1, 1, -1),),
    (2, 2): ((1, 2, -1), (0, 0, 0), (2, 0, -1), (0, 1, 0)),
    (3, 0): ((2, 1, -1),),
    (3, 1): ((1, 0, 0),),
}
AFTER = (
    (2, 2, -1), (1, 1, 0), (0, 2, 0), (3, 0, -1), (3, 1, -1), (0, 0, 1), (0, 1, 1), (3, 2, -1), (1, 2, 0), (2, 0, 0),
    (2, 1, 0), (1, 0, 1), (3, 0, 0), (2, 2, 0), (3, 2, 0), (1, 1, 1), (3, 1, 0), "spread", (2, 1, 1), (0, 2, 1),
    (2, 0, 1), (3, 0, 1), (1, 2, 1), (3, 2, 1), (2, 2, 1), (3, 1, 1),
)
LAST = (
    (0, 0), (0, 1), (1, 0), (0, 2), (2, 1), (1, 1), (2, 0), (1, 2), (3, 0), (3, 2), (2, 2), (3, 1),
)


def ldl(gram):
    row = lax.broadcasted_iota(jnp.int32, (8, 8), 0)
    col = lax.broadcasted_iota(jnp.int32, (8, 8), 1)
    eye = (row == col).astype(F32)
    a = jnp.where((row == 7) | (col == 7), eye, gram)
    inv, inv_t = eye, eye
    for j in range(6):
        piv = a[j : j + 1, j : j + 1]
        f_col = jnp.where(row[:, :1] > j, a[:, j : j + 1] / piv, 0.0)
        f_row = jnp.where(col[:1, :] > j, a[j : j + 1, :] / piv, 0.0)
        inv = inv - f_col * inv[j : j + 1, :]
        inv_t = inv_t - inv_t[:, j : j + 1] * f_row
        a = a - f_col * a[j : j + 1, :]
    diag = jnp.sum(a * eye, axis=1, keepdims=True)
    return inv, inv_t, diag


def solve(factor, rhs):
    inv, inv_t, diag = factor
    mid = inv[:, 0:1] * rhs[0:1, :]
    for j in range(1, 7):
        mid = mid + inv[:, j : j + 1] * rhs[j : j + 1, :]
    mid = mid / diag
    out = inv_t[:, 0:1] * mid[0:1, :]
    for j in range(1, 7):
        out = out + inv_t[:, j : j + 1] * mid[j : j + 1, :]
    return out


def kernel(
    scale,
    sig_hbm, prof_hbm, expr_hbm, dos_hbm,
    inter_ref, props_ref,
    e_v, d_v, d_t, des, sig_ref, prof_ref, sig_sc, m_sc, acc, rc, r1, r2, r3,
    pbuf, rsnd, rrcv, gsnd, grcv, corr_sc, pp_sc, py_sc, fac_sc, tsrc, trcv, tbuf, mix,
    e_sem, d_sem, i_sem, sent, g_r, x_r, p_r, c_r, h_r, t_r, u_r,
):
    s_dev, g_dev = e_v.shape
    quarter = s_dev // N_GENE
    half = quarter // 2
    n_cols = g_dev // N_CHUNK
    n_tiles = g_dev // 128
    per_chunk = n_cols // 128
    types = 7
    g = lax.axis_index("gene")
    s = lax.axis_index("sample")
    y, z, c = s // 4, (s // 2) % 2, s % 2
    b = y // 2
    a = (y + b) % 2
    place = {"a": a, "b": b, "z": z}
    other = {
        "a": (2 * b + (1 - a + b) % 2) * 4 + z * 2 + c,
        "b": (2 * (1 - b) + (a + 1 - b) % 2) * 4 + z * 2 + c,
        "z": s + 2 - 4 * z,
    }
    core = s + 1 - 2 * c

    def gene_of(d):
        return {"gene": (g + d) % N_GENE}

    def sample_of(d):
        return {"sample": (s + d) % N_SAMPLE}

    def quarter_of(d):
        return (g + N_GENE - d) % N_GENE

    def load(d, h):
        source = pl.ds(pl.multiple_of(quarter_of(d) * quarter + h * half, half), half)
        target = pl.ds(pl.multiple_of(d * quarter + h * half, half), half)
        return pltpu.make_async_copy(expr_hbm.at[source, :], e_v.at[target, :], e_sem.at[d, h])

    def load_dosage(d):
        source = pl.ds(pl.multiple_of(quarter_of(d) * quarter, quarter), quarter)
        return pltpu.make_async_copy(dos_hbm.at[source, :], d_v.at[pl.ds(d * quarter, quarter), :], d_sem.at[d])

    def remote(src, dst, recv, device):
        return pltpu.make_async_remote_copy(
            src_ref=src, dst_ref=dst, send_sem=sent, recv_sem=recv, device_id=device, device_id_type=MESH
        )

    sig_copy = pltpu.make_async_copy(sig_hbm, sig_ref, i_sem.at[0])
    prof_copy = pltpu.make_async_copy(prof_hbm, prof_ref, i_sem.at[1])
    sig_copy.start()
    prof_copy.start()
    for h in range(2):
        load(1, h).start()

    barrier = pltpu.get_barrier_semaphore()
    for d in range(1, N_GENE):
        pl.semaphore_signal(barrier, inc=1, device_id=gene_of(d), device_id_type=MESH)
    for d in range(1, N_SAMPLE):
        pl.semaphore_signal(barrier, inc=1, device_id=sample_of(d), device_id_type=MESH)

    n_sig = sig_ref.shape[1]
    sig_sc[...] = jnp.full(sig_sc.shape, -1, jnp.int32)
    sig_copy.wait()
    prof_copy.wait()
    for d in (2, 3, 0):
        for h in range(2):
            load(d, h).start()
    for d in range(N_GENE):
        load_dosage(d).start()
    sig_sc[0:1, 0:n_sig] = sig_ref[...]
    cols = []
    for t in range(sig_sc.shape[1] // 128):
        line = sig_sc[0:1, 128 * t : 128 * t + 128].astype(F32)
        cols.append(jnp.transpose(jnp.broadcast_to(line, (128, 128))))
    lane = lax.broadcasted_iota(jnp.int32, (128, 128), 1) + g * g_dev
    m_sc[...] = jnp.zeros(m_sc.shape, F32)
    for t in range(n_tiles):
        ids = (lane + 128 * t).astype(F32)
        hit = jnp.zeros((128, 128), F32)
        for column in cols:
            hit = jnp.where(column == ids, 1.0, hit)
        member = jnp.max(hit, axis=0, keepdims=True)
        m_sc[0:types, 128 * t : 128 * t + 128] = prof_ref[:, 128 * t : 128 * t + 128] * member
    masked = m_sc[...]
    gsnd[...] = jnp.zeros(gsnd.shape, F32)
    gsnd[:, 0:8] = lax.dot_general(masked, masked, NT, precision=HIGH, preferred_element_type=F32)
    top = masked.astype(BF16).astype(F32)
    rest = masked - top
    mid = rest.astype(BF16).astype(F32)
    m3 = jnp.concatenate([top, mid, rest - mid], axis=0).astype(BF16)

    def gram_copy(d):
        return remote(gsnd, grcv.at[d - 1], g_r.at[d - 1], gene_of(d))

    def rhs_copy(d, h):
        return remote(rsnd.at[d, h], rrcv.at[d - 1, h], x_r.at[d - 1, h], gene_of(d))

    def rhs_half(i, carry):
        d, h = N_GENE - 1 - i // 2, i % 2
        at = (N_GENE - d) % N_GENE
        load(at, h).wait()
        rows = pl.ds(pl.multiple_of(at * quarter + h * half, half), half)
        part = lax.dot_general(m3, e_v[rows, :], NT, preferred_element_type=F32)
        rsnd[d, h] = part[0:8] + part[8:16] + part[16:24]

        @pl.when(i == 0)
        def _():
            pl.semaphore_wait(barrier, N_GENE - 1 + N_SAMPLE - 1)
            for peer in range(1, N_GENE):
                gram_copy(peer).start()

        @pl.when(d > 0)
        def _():
            rhs_copy(d, h).start()

        return carry

    lax.fori_loop(0, 2 * N_GENE, rhs_half, 0)

    for d in range(N_GENE):
        load_dosage(d).wait()
    for i in range(s_dev // 128):
        piece = d_v[128 * i : 128 * i + 128, :].astype(F32).astype(BF16)
        d_t[:, 128 * i : 128 * i + 128] = jnp.transpose(piece)
    corr_sc[...] = jnp.zeros(corr_sc.shape, F32)
    pp_sc[...] = jnp.zeros(pp_sc.shape, F32)
    gram = gsnd[:, 0:8]
    for d in range(1, N_GENE):
        gram_copy(d).wait_recv()
        gram = gram + grcv[d - 1, :, 0:8]
    factor = ldl(gram)
    for d in (3, 2, 1):
        for h in range(2):
            rhs_copy(d, h).wait_recv()
    for h in range(2):
        pbuf[g, :, h * half : (h + 1) * half] = solve(factor, rsnd[0, h] + rrcv[2, h] + rrcv[1, h] + rrcv[0, h])

    def props_copy(d):
        return remote(pbuf.at[g], pbuf.at[g], p_r.at[d - 1], gene_of(d))

    for d in (2, 1, 3):
        props_copy(d).start()

    def span_of(d):
        return slice(d * quarter, (d + 1) * quarter)

    def design(d):
        props = pbuf[quarter_of(d)]
        props_ref[:, pl.ds(pl.multiple_of(quarter_of(d) * quarter, quarter), quarter)] = props[0:types]
        top = props.astype(BF16).astype(F32)
        des[896:912, span_of(d)] = jnp.concatenate([top, props - top], axis=0).astype(BF16)
        for k in range(types):
            lo, hi = [part for part in PARTS if part[0] <= k < part[1]][0]
            wide = jnp.broadcast_to(top[k : k + 1, :], (16, quarter)).astype(BF16)
            for bb in range(2):
                for aa in range(2):
                    for zz in range(2):
                        source = ((2 * bb + (aa + bb) % 2) * 2 + zz) * 16
                        target = lo * 128 + (((bb * 2 + aa) * 2 + zz) * (hi - lo) + k - lo) * 16
                        des[target : target + 16, span_of(d)] = d_t[source : source + 16, span_of(d)] * wide

    def small_term(d):
        span = pl.ds(pl.multiple_of(d * quarter, quarter), quarter)
        props = pbuf[quarter_of(d)]
        top = props.astype(BF16).astype(F32)
        highs, lows = [], []
        for k in range(types):
            weight = jnp.broadcast_to(top[k : k + 1, :], (8, quarter)) * props
            high = weight.astype(BF16).astype(F32)
            highs.append(high)
            lows.append(weight - high)
        w = jnp.concatenate(highs + lows, axis=0).astype(BF16)
        corr = lax.dot_general(d_t[:, span], w, NT, preferred_element_type=F32)
        both = des[896:912, span]
        pp = lax.dot_general(both, both, NT, preferred_element_type=F32)
        corr_sc[:, 0 : 16 * types] += corr
        pp_sc[:, 0:16] += pp[0:8] + pp[8:16]

    def term(n, part, first):
        columns = pl.ds(pl.multiple_of(n * n_cols, n_cols), n_cols)
        span = slice(0, quarter) if first else slice(quarter, s_dev)
        lo, hi = PARTS[part]
        size = 128 * (hi - lo)
        last = part == len(PARTS) - 1
        rows = slice(128 * lo, 128 * hi + (16 if last else 0))
        value = jnp.dot(des[rows, span], e_v[span, columns], preferred_element_type=F32)
        body = value[0:size].reshape(acc[part].shape[1:])
        acc[part][n] = body if first else acc[part][n] + body
        if last:
            tail = value[size : size + 8] + value[size + 8 : size + 16]
            py_sc[n] = tail if first else py_sc[n] + tail

    def core_copy(n, part):
        return remote(
            acc[part].at[n, :, :, :, :, 1 - c], rc[part].at[n], c_r.at[n, part], {"sample": core}
        )

    def halving(n, part, step):
        axes = ORDERS[n][part]
        kept = {axis: place[axis] for axis in axes[:step]}
        axis = axes[step]

        def block(fixed):
            return (n,) + tuple(fixed.get(name, slice(None)) for name in "baz") + (slice(None), c)

        landing = ((r1, r2, r3)[step])[part].at[n]
        copy = remote(
            acc[part].at[block({**kept, axis: 1 - place[axis]})],
            landing,
            h_r.at[n, part, step],
            {"sample": other[axis]},
        )
        return copy, block({**kept, axis: place[axis]}), landing

    def advance(n, part, step):
        if step < 0:
            core_copy(n, part).wait_recv()
            acc[part][n, :, :, :, :, c] += rc[part][n]
        else:
            copy, kept, landing = halving(n, part, step)
            copy.wait_recv()
            acc[part][kept] += landing[...]
        halving(n, part, step + 1)[0].start()

    def tile_copy(d):
        return remote(tsrc.at[(s + d) % N_SAMPLE], trcv.at[d], t_r, sample_of(d))

    def spread_copy(d):
        return remote(tbuf.at[0], tbuf.at[d], u_r, sample_of(d))

    def start_tiles(d, carry):
        tile_copy(d).start()
        return carry

    def wait_tiles(buffer, recv):
        remote(tsrc.at[1:N_SAMPLE], buffer.at[1:N_SAMPLE], recv, sample_of(1)).wait_recv()

    def start_spread(d, carry):
        spread_copy(d).start()
        return carry

    spot = lax.broadcasted_iota(jnp.int32, (8, 128), 1)
    n_kj = 8 * types

    def send_tiles():
        pp = pp_sc[...]
        pp = pltpu.roll(pp + pltpu.roll(pp, 120, 1), n_kj, 1)
        for i in range(N_SAMPLE):
            corr = corr_sc[8 * i : 8 * i + 8, :]
            corr = corr + pltpu.roll(corr, 128 - n_kj, 1)
            at = 64 * i
            py = py_sc[at // n_cols, :, at % n_cols // 128 * 128 : at % n_cols // 128 * 128 + 128]
            if i % 2 == 0:
                py = pltpu.roll(py, 64, 1)
            tsrc[i] = jnp.where(spot < n_kj, corr, jnp.where(spot < 64, pp, py))
        lax.fori_loop(1, N_SAMPLE, start_tiles, 0)

    def spread_tiles():
        wait_tiles(trcv, t_r)
        total = tsrc[s]
        for d in range(1, N_SAMPLE):
            total = total + trcv[d]
        tbuf[0] = total
        lax.fori_loop(1, N_SAMPLE, start_spread, 0)
        corr_sc[0:8, :] = total
        inv, inv_t, diag = ldl(pltpu.roll(total, 128 - n_kj, 1)[:, 0:8])
        fac_sc[0, :, 0:8] = inv
        fac_sc[1, :, 0:8] = inv_t
        fac_sc[2, :, 0:1] = diag

    def solve_coef():
        wait_tiles(tbuf, u_r)
        factor = fac_sc[0, :, 0:8], fac_sc[1, :, 0:8], fac_sc[2, :, 0:1]
        own = [tbuf[(s + N_SAMPLE - i) % N_SAMPLE] for i in range(N_SAMPLE)]
        tiles = [jnp.where(spot < 64, pltpu.roll(own[2 * i], 64, 1), own[2 * i + 1]) for i in range(n_tiles)]
        m_sc[...] = solve(factor, jnp.concatenate(tiles, axis=1))

    def finish(n, part):
        corr = corr_sc[0:8, :]
        coef = m_sc[:, n * n_cols : (n + 1) * n_cols]
        copy, kept, landing = halving(n, part, 2)
        copy.wait_recv()
        value = acc[part][kept] + landing[...]
        for k in range(*PARTS[part]):
            out = value[k - PARTS[part][0]]
            for j in range(types):
                out = out - corr[:, 8 * k + j : 8 * k + j + 1] * coef[j : j + 1, :]
            out = out * scale
            for i in range(per_chunk):
                mix[n * per_chunk + i, pl.ds(k, 8, stride=types), :] = out[:, 128 * i : 128 * i + 128]

    design(0)

    def own(n, carry):
        for part in range(3):
            term(n, part, True)
        return carry

    lax.fori_loop(0, N_CHUNK, own, 0)
    small_term(0)
    for d in (1, 3, 2):
        props_copy(d).wait_recv()
        design(d)

    def others(n, carry):
        for part in range(3):
            term(n, part, False)
            core_copy(n, part).start()
            if part == 2:
                @pl.when(n > 0)
                def _():
                    small_term(n)

            for chunk in range(N_CHUNK):
                events = DURING.get((chunk, part), ())
                if events:
                    @pl.when(n == chunk)
                    def _(events=events):
                        for event in events:
                            advance(*event)

        return carry

    lax.fori_loop(0, N_CHUNK, others, 0)
    send_tiles()
    for event in AFTER:
        if event == "spread":
            spread_tiles()
        else:
            advance(*event)
    solve_coef()
    left = [3] * N_CHUNK
    for n, part in LAST:
        finish(n, part)
        left[n] -= 1
        if left[n] == 0:
            for i in range(n * per_chunk, (n + 1) * per_chunk):
                inter_ref[:, 128 * i : 128 * i + 128] = mix[i]

    for d in range(1, N_GENE):
        gram_copy(d).wait_send()
        for h in range(2):
            rhs_copy(d, h).wait_send()
        props_copy(d).wait_send()
    for n in range(N_CHUNK):
        for part in range(3):
            core_copy(n, part).wait_send()
            for step in range(3):
                halving(n, part, step)[0].wait_send()

    def drain_tiles(d, carry):
        tile_copy(d).wait_send()
        spread_copy(d).wait_send()
        return carry

    lax.fori_loop(1, N_SAMPLE, drain_tiles, 0)


def store(inter_ref, props_ref, inter_out, props_out, sem):
    copies = (
        pltpu.make_async_copy(inter_ref, inter_out, sem.at[0]),
        pltpu.make_async_copy(props_ref, props_out, sem.at[1]),
    )
    for copy in copies:
        copy.start()
    for copy in copies:
        copy.wait()


def local(expression, profile, dosage, signature):
    s_dev, g_dev = expression.shape
    v_dev = dosage.shape[1]
    types = profile.shape[1]
    quarter, n_cols = s_dev // N_GENE, g_dev // N_CHUNK
    scale = 1.0 / math.sqrt(s_dev * N_SAMPLE)
    sig_cols = -(-signature.shape[0] // 128) * 128
    sizes = [hi - lo for lo, hi in PARTS]
    vmem, dma = pltpu.VMEM, pltpu.SemaphoreType.DMA
    inter, props_t = pl.pallas_call(
        functools.partial(kernel, scale),
        out_shape=(
            vmem((v_dev * types // N_SAMPLE, g_dev), F32),
            vmem((types, s_dev), F32),
        ),
        in_specs=[
            pl.BlockSpec(memory_space=pl.ANY),
            pl.BlockSpec(memory_space=pl.ANY),
            pl.BlockSpec(memory_space=pl.ANY),
            pl.BlockSpec(memory_space=pl.ANY),
        ],
        out_specs=(pl.BlockSpec(memory_space=pltpu.VMEM), pl.BlockSpec(memory_space=pltpu.VMEM)),
        scratch_shapes=[
            vmem((s_dev, g_dev), BF16),
            vmem((s_dev, v_dev), jnp.int32),
            vmem((v_dev, s_dev), BF16),
            vmem((v_dev * types + 16, s_dev), BF16),
            vmem((1, signature.shape[0]), jnp.int32),
            vmem((types, g_dev), F32),
            vmem((1, sig_cols), jnp.int32),
            vmem((8, g_dev), F32),
            [vmem((N_CHUNK, 2, 2, 2, k, 2, 8, n_cols), F32) for k in sizes],
            [vmem((N_CHUNK, 2, 2, 2, k, 8, n_cols), F32) for k in sizes],
            [vmem((N_CHUNK, 2, 2, k, 8, n_cols), F32) for k in sizes],
            [vmem((N_CHUNK, 2, k, 8, n_cols), F32) for k in sizes],
            [vmem((N_CHUNK, k, 8, n_cols), F32) for k in sizes],
            vmem((N_GENE, 8, quarter), F32),
            vmem((N_GENE, 2, 8, quarter // 2), F32),
            vmem((N_GENE - 1, 2, 8, quarter // 2), F32),
            vmem((8, 128), F32),
            vmem((N_GENE - 1, 8, 128), F32),
            vmem((v_dev, 128), F32),
            vmem((8, 128), F32),
            vmem((N_CHUNK, 8, n_cols), F32),
            vmem((3, 8, 128), F32),
            vmem((N_SAMPLE, 8, 128), F32),
            vmem((N_SAMPLE, 8, 128), F32),
            vmem((N_SAMPLE, 8, 128), F32),
            vmem((g_dev // 128, 8 * types, 128), F32),
            dma((N_GENE, 2)),
            dma((N_GENE,)),
            dma((2,)),
            dma,
            dma((N_GENE - 1,)),
            dma((N_GENE - 1, 2)),
            dma((N_GENE - 1,)),
            dma((N_CHUNK, 3)),
            dma((N_CHUNK, 3, 3)),
            dma,
            dma,
        ],
        compiler_params=pltpu.CompilerParams(
            collective_id=0, has_side_effects=True, vmem_limit_bytes=VMEM_BYTES
        ),
        name="eqtl",
    )(signature.reshape(1, -1), profile.T, expression, dosage)
    inter, props_t = pl.pallas_call(
        store,
        out_shape=(
            jax.ShapeDtypeStruct(inter.shape, F32),
            jax.ShapeDtypeStruct(props_t.shape, F32),
        ),
        in_specs=[pl.BlockSpec(memory_space=pltpu.VMEM)] * 2,
        out_specs=(pl.BlockSpec(memory_space=pl.ANY), pl.BlockSpec(memory_space=pl.ANY)),
        scratch_shapes=[dma((2,))],
        compiler_params=pltpu.CompilerParams(vmem_limit_bytes=8 * 1024 * 1024),
        name="store",
    )(inter, props_t)
    return inter, props_t.T


def solution(mesh):
    placed = (P("sample", "gene"), P("gene", None), P("sample", "variant"), P())
    return jax.shard_map(
        local,
        mesh=mesh,
        in_specs=placed,
        out_specs=(P(("variant", "sample"), "gene"), P("sample", None)),
        check_vma=False,
    )
```

```python
import functools
import math

import jax
import jax.numpy as jnp
from jax import lax
from jax.experimental import pallas as pl
from jax.experimental.pallas import tpu as pltpu
from jax.sharding import PartitionSpec as P

MESH = pl.DeviceIdType.MESH
HIGH = lax.Precision.HIGHEST
F32, BF16 = jnp.float32, jnp.bfloat16
NT = (((1,), (1,)), ((), ()))
N_GENE = 4
N_SAMPLE = 16
N_CHUNK = 4
VMEM_BYTES = 62_000_000
PARTS = ((0, 2), (2, 4), (4, 7))
ORDERS = (
    ("bza", "zba", "baz"),
    ("abz", "zba", "zab"),
    ("azb", "baz", "bza"),
    ("abz", "azb", "zba"),
)
AFTER = (
    (0, 0, 0), (0, 1, 0), (1, 0, 0), (1, 1, 0), (3, 0, -1), (3, 1, -1), (0, 2, 0), (3, 2, -1), (0, 1, 1), (2, 0, 0),
    (1, 2, 0), (2, 1, 0), "spread", (0, 0, 1), (3, 0, 0), (2, 2, 0), (3, 1, 0), (1, 0, 1), (3, 2, 0), (0, 2, 1),
    (1, 1, 1), (2, 0, 1), (3, 0, 1), (2, 2, 1), (1, 2, 1), (3, 1, 1), (3, 2, 1), (2, 1, 1),
)
LAST = (
    (1, 0), (2, 0), (0, 0), (0, 1), (1, 1), (0, 2), (3, 0), (2, 2), (1, 2), (3, 1), (2, 1), (3, 2),
)


def ldl(gram):
    row = lax.broadcasted_iota(jnp.int32, (8, 8), 0)
    col = lax.broadcasted_iota(jnp.int32, (8, 8), 1)
    eye = (row == col).astype(F32)
    a = jnp.where((row == 7) | (col == 7), eye, gram)
    inv, inv_t = eye, eye
    for j in range(6):
        piv = a[j : j + 1, j : j + 1]
        f_col = jnp.where(row[:, :1] > j, a[:, j : j + 1] / piv, 0.0)
        f_row = jnp.where(col[:1, :] > j, a[j : j + 1, :] / piv, 0.0)
        inv = inv - f_col * inv[j : j + 1, :]
        inv_t = inv_t - inv_t[:, j : j + 1] * f_row
        a = a - f_col * a[j : j + 1, :]
    diag = jnp.sum(a * eye, axis=1, keepdims=True)
    return inv, inv_t, diag


def solve(factor, rhs):
    inv, inv_t, diag = factor
    mid = inv[:, 0:1] * rhs[0:1, :]
    for j in range(1, 7):
        mid = mid + inv[:, j : j + 1] * rhs[j : j + 1, :]
    mid = mid / diag
    out = inv_t[:, 0:1] * mid[0:1, :]
    for j in range(1, 7):
        out = out + inv_t[:, j : j + 1] * mid[j : j + 1, :]
    return out


def kernel(
    scale,
    sig_hbm, prof_hbm, expr_hbm, dos_hbm,
    inter_ref, props_ref,
    e_v, d_v, d_t, des, sig_ref, prof_ref, sig_sc, m_sc, acc, rc, r1, r2, r3,
    pbuf, rsnd, rrcv, gsnd, grcv, corr_sc, pp_sc, py_sc, fac_sc, tsrc, trcv, tbuf, mix,
    e_sem, d_sem, i_sem, sent, g_r, x_r, p_r, c_r, h_r, t_r, u_r,
):
    s_dev, g_dev = e_v.shape
    quarter = s_dev // N_GENE
    half = quarter // 2
    n_cols = g_dev // N_CHUNK
    n_tiles = g_dev // 128
    per_chunk = n_cols // 128
    types = 7
    g = lax.axis_index("gene")
    s = lax.axis_index("sample")
    y, z, c = s // 4, (s // 2) % 2, s % 2
    b = y // 2
    a = (y + b) % 2
    place = {"a": a, "b": b, "z": z}
    other = {
        "a": (2 * b + (1 - a + b) % 2) * 4 + z * 2 + c,
        "b": (2 * (1 - b) + (a + 1 - b) % 2) * 4 + z * 2 + c,
        "z": s + 2 - 4 * z,
    }
    core = s + 1 - 2 * c

    def gene_of(d):
        return {"gene": (g + d) % N_GENE}

    def sample_of(d):
        return {"sample": (s + d) % N_SAMPLE}

    def quarter_of(d):
        return (g + N_GENE - d) % N_GENE

    def load(d, h):
        source = pl.ds(pl.multiple_of(quarter_of(d) * quarter + h * half, half), half)
        target = pl.ds(pl.multiple_of(d * quarter + h * half, half), half)
        return pltpu.make_async_copy(expr_hbm.at[source, :], e_v.at[target, :], e_sem.at[d, h])

    def load_dosage(d):
        source = pl.ds(pl.multiple_of(quarter_of(d) * quarter, quarter), quarter)
        return pltpu.make_async_copy(dos_hbm.at[source, :], d_v.at[pl.ds(d * quarter, quarter), :], d_sem.at[d])

    def remote(src, dst, recv, device):
        return pltpu.make_async_remote_copy(
            src_ref=src, dst_ref=dst, send_sem=sent, recv_sem=recv, device_id=device, device_id_type=MESH
        )

    sig_copy = pltpu.make_async_copy(sig_hbm, sig_ref, i_sem.at[0])
    prof_copy = pltpu.make_async_copy(prof_hbm, prof_ref, i_sem.at[1])
    sig_copy.start()
    prof_copy.start()
    for h in range(2):
        load(1, h).start()

    barrier = pltpu.get_barrier_semaphore()
    for d in range(1, N_GENE):
        pl.semaphore_signal(barrier, inc=1, device_id=gene_of(d), device_id_type=MESH)
    for d in range(1, N_SAMPLE):
        pl.semaphore_signal(barrier, inc=1, device_id=sample_of(d), device_id_type=MESH)

    n_sig = sig_ref.shape[1]
    sig_sc[...] = jnp.full(sig_sc.shape, -1, jnp.int32)
    sig_copy.wait()
    prof_copy.wait()
    for d in (2, 3, 0):
        for h in range(2):
            load(d, h).start()
    for d in range(N_GENE):
        load_dosage(d).start()
    sig_sc[0:1, 0:n_sig] = sig_ref[...]
    cols = []
    for t in range(sig_sc.shape[1] // 128):
        line = sig_sc[0:1, 128 * t : 128 * t + 128].astype(F32)
        cols.append(jnp.transpose(jnp.broadcast_to(line, (128, 128))))
    lane = lax.broadcasted_iota(jnp.int32, (128, 128), 1) + g * g_dev
    m_sc[...] = jnp.zeros(m_sc.shape, F32)
    for t in range(n_tiles):
        ids = (lane + 128 * t).astype(F32)
        hit = jnp.zeros((128, 128), F32)
        for column in cols:
            hit = jnp.where(column == ids, 1.0, hit)
        member = jnp.max(hit, axis=0, keepdims=True)
        m_sc[0:types, 128 * t : 128 * t + 128] = prof_ref[:, 128 * t : 128 * t + 128] * member
    masked = m_sc[...]
    gsnd[...] = jnp.zeros(gsnd.shape, F32)
    gsnd[:, 0:8] = lax.dot_general(masked, masked, NT, precision=HIGH, preferred_element_type=F32)
    top = masked.astype(BF16).astype(F32)
    rest = masked - top
    mid = rest.astype(BF16).astype(F32)
    m3 = jnp.concatenate([top, mid, rest - mid], axis=0).astype(BF16)

    def gram_copy(d):
        return remote(gsnd, grcv.at[d - 1], g_r.at[d - 1], gene_of(d))

    def rhs_copy(d):
        return remote(rsnd.at[d], rrcv.at[d - 1], x_r.at[d - 1], gene_of(d))

    def rhs_quarter(i, carry):
        d = N_GENE - 1 - i
        at = (N_GENE - d) % N_GENE
        for h in range(2):
            load(at, h).wait()
        for h in range(2):
            rows = pl.ds(pl.multiple_of(at * quarter + h * half, half), half)
            part = lax.dot_general(m3, e_v[rows, :], NT, preferred_element_type=F32)
            rsnd[d, :, h * half : (h + 1) * half] = part[0:8] + part[8:16] + part[16:24]

        @pl.when(i == 0)
        def _():
            pl.semaphore_wait(barrier, N_GENE - 1 + N_SAMPLE - 1)
            for peer in range(1, N_GENE):
                gram_copy(peer).start()

        @pl.when(d > 0)
        def _():
            rhs_copy(d).start()

        return carry

    lax.fori_loop(0, N_GENE, rhs_quarter, 0)

    for d in range(N_GENE):
        load_dosage(d).wait()
    for i in range(s_dev // 128):
        piece = d_v[128 * i : 128 * i + 128, :].astype(F32).astype(BF16)
        d_t[:, 128 * i : 128 * i + 128] = jnp.transpose(piece)
    corr_sc[...] = jnp.zeros(corr_sc.shape, F32)
    pp_sc[...] = jnp.zeros(pp_sc.shape, F32)
    gram = gsnd[:, 0:8]
    for d in range(1, N_GENE):
        gram_copy(d).wait_recv()
        gram = gram + grcv[d - 1, :, 0:8]
    factor = ldl(gram)
    for d in (3, 2, 1):
        rhs_copy(d).wait_recv()
    pbuf[g] = solve(factor, rsnd[0] + rrcv[2] + rrcv[1] + rrcv[0])

    def props_copy(d):
        return remote(pbuf.at[g], pbuf.at[g], p_r.at[d - 1], gene_of(d))

    for d in (2, 1, 3):
        props_copy(d).start()

    def span_of(d):
        return slice(d * quarter, (d + 1) * quarter)

    def design(d):
        props = pbuf[quarter_of(d)]
        props_ref[:, pl.ds(pl.multiple_of(quarter_of(d) * quarter, quarter), quarter)] = props[0:types]
        top = props.astype(BF16).astype(F32)
        des[896:912, span_of(d)] = jnp.concatenate([top, props - top], axis=0).astype(BF16)
        for k in range(types):
            lo, hi = [part for part in PARTS if part[0] <= k < part[1]][0]
            wide = jnp.broadcast_to(top[k : k + 1, :], (16, quarter)).astype(BF16)
            for bb in range(2):
                for aa in range(2):
                    for zz in range(2):
                        source = ((2 * bb + (aa + bb) % 2) * 2 + zz) * 16
                        target = lo * 128 + (((bb * 2 + aa) * 2 + zz) * (hi - lo) + k - lo) * 16
                        des[target : target + 16, span_of(d)] = d_t[source : source + 16, span_of(d)] * wide

    def small_term(d):
        span = pl.ds(pl.multiple_of(d * quarter, quarter), quarter)
        props = pbuf[quarter_of(d)]
        top = props.astype(BF16).astype(F32)
        highs, lows = [], []
        for k in range(types):
            weight = jnp.broadcast_to(top[k : k + 1, :], (8, quarter)) * props
            high = weight.astype(BF16).astype(F32)
            highs.append(high)
            lows.append(weight - high)
        w = jnp.concatenate(highs + lows, axis=0).astype(BF16)
        corr = lax.dot_general(d_t[:, span], w, NT, preferred_element_type=F32)
        both = des[896:912, span]
        pp = lax.dot_general(both, both, NT, preferred_element_type=F32)
        corr_sc[:, 0 : 16 * types] += corr
        pp_sc[:, 0:16] += pp[0:8] + pp[8:16]

    def term(n, first):
        columns = pl.ds(pl.multiple_of(n * n_cols, n_cols), n_cols)
        span = slice(0, quarter) if first else slice(quarter, s_dev)
        value = jnp.dot(des[:, span], e_v[span, columns], preferred_element_type=F32)
        for part, (lo, hi) in enumerate(PARTS):
            body = value[128 * lo : 128 * hi].reshape(acc[part].shape[1:])
            acc[part][n] = body if first else acc[part][n] + body
        tail = value[896:904] + value[904:912]
        py_sc[n] = tail if first else py_sc[n] + tail

    def core_copy(n, part):
        return remote(
            acc[part].at[n, :, :, :, :, 1 - c], rc[part].at[n], c_r.at[n, part], {"sample": core}
        )

    def halving(n, part, step):
        axes = ORDERS[n][part]
        kept = {axis: place[axis] for axis in axes[:step]}
        axis = axes[step]

        def block(fixed):
            return (n,) + tuple(fixed.get(name, slice(None)) for name in "baz") + (slice(None), c)

        landing = ((r1, r2, r3)[step])[part].at[n]
        copy = remote(
            acc[part].at[block({**kept, axis: 1 - place[axis]})],
            landing,
            h_r.at[n, part, step],
            {"sample": other[axis]},
        )
        return copy, block({**kept, axis: place[axis]}), landing

    def advance(n, part, step):
        if step < 0:
            core_copy(n, part).wait_recv()
            acc[part][n, :, :, :, :, c] += rc[part][n]
        else:
            copy, kept, landing = halving(n, part, step)
            copy.wait_recv()
            acc[part][kept] += landing[...]
        halving(n, part, step + 1)[0].start()

    def tile_copy(d):
        return remote(tsrc.at[(s + d) % N_SAMPLE], trcv.at[d], t_r, sample_of(d))

    def spread_copy(d):
        return remote(tbuf.at[0], tbuf.at[d], u_r, sample_of(d))

    def start_tiles(d, carry):
        tile_copy(d).start()
        return carry

    def wait_tiles(buffer, recv):
        remote(tsrc.at[1:N_SAMPLE], buffer.at[1:N_SAMPLE], recv, sample_of(1)).wait_recv()

    def start_spread(d, carry):
        spread_copy(d).start()
        return carry

    spot = lax.broadcasted_iota(jnp.int32, (8, 128), 1)
    n_kj = 8 * types

    def send_tiles():
        pp = pp_sc[...]
        pp = pltpu.roll(pp + pltpu.roll(pp, 120, 1), n_kj, 1)
        for i in range(N_SAMPLE):
            corr = corr_sc[8 * i : 8 * i + 8, :]
            corr = corr + pltpu.roll(corr, 128 - n_kj, 1)
            at = 64 * i
            py = py_sc[at // n_cols, :, at % n_cols // 128 * 128 : at % n_cols // 128 * 128 + 128]
            if i % 2 == 0:
                py = pltpu.roll(py, 64, 1)
            tsrc[i] = jnp.where(spot < n_kj, corr, jnp.where(spot < 64, pp, py))
        lax.fori_loop(1, N_SAMPLE, start_tiles, 0)

    def spread_tiles():
        wait_tiles(trcv, t_r)
        total = tsrc[s]
        for d in range(1, N_SAMPLE):
            total = total + trcv[d]
        tbuf[0] = total
        lax.fori_loop(1, N_SAMPLE, start_spread, 0)
        corr_sc[0:8, :] = total
        inv, inv_t, diag = ldl(pltpu.roll(total, 128 - n_kj, 1)[:, 0:8])
        fac_sc[0, :, 0:8] = inv
        fac_sc[1, :, 0:8] = inv_t
        fac_sc[2, :, 0:1] = diag

    def solve_coef():
        wait_tiles(tbuf, u_r)
        factor = fac_sc[0, :, 0:8], fac_sc[1, :, 0:8], fac_sc[2, :, 0:1]
        own = [tbuf[(s + N_SAMPLE - i) % N_SAMPLE] for i in range(N_SAMPLE)]
        tiles = [jnp.where(spot < 64, pltpu.roll(own[2 * i], 64, 1), own[2 * i + 1]) for i in range(n_tiles)]
        m_sc[...] = solve(factor, jnp.concatenate(tiles, axis=1))

    def finish(n, part):
        corr = corr_sc[0:8, :]
        coef = m_sc[:, n * n_cols : (n + 1) * n_cols]
        copy, kept, landing = halving(n, part, 2)
        copy.wait_recv()
        value = acc[part][kept] + landing[...]
        for k in range(*PARTS[part]):
            out = value[k - PARTS[part][0]]
            for j in range(types):
                out = out - corr[:, 8 * k + j : 8 * k + j + 1] * coef[j : j + 1, :]
            out = out * scale
            for i in range(per_chunk):
                mix[n * per_chunk + i, pl.ds(k, 8, stride=types), :] = out[:, 128 * i : 128 * i + 128]

    design(0)

    def own(n, carry):
        term(n, True)
        return carry

    lax.fori_loop(0, N_CHUNK, own, 0)
    small_term(0)
    for d in (1, 3, 2):
        props_copy(d).wait_recv()
        design(d)

    def others(n, carry):
        term(n, False)
        for part in range(3):
            core_copy(n, part).start()

        @pl.when(n > 0)
        def _():
            small_term(n)

        @pl.when(n == N_CHUNK - 1)
        def _():
            send_tiles()

        for chunk in range(1, N_CHUNK):
            @pl.when(n == chunk)
            def _(chunk=chunk):
                for part in range(3):
                    advance(chunk - 1, part, -1)

        return carry

    lax.fori_loop(0, N_CHUNK, others, 0)
    for event in AFTER:
        if event == "spread":
            spread_tiles()
        else:
            advance(*event)
    solve_coef()
    left = [3] * N_CHUNK
    for n, part in LAST:
        finish(n, part)
        left[n] -= 1
        if left[n] == 0:
            for i in range(n * per_chunk, (n + 1) * per_chunk):
                inter_ref[:, 128 * i : 128 * i + 128] = mix[i]

    for d in range(1, N_GENE):
        gram_copy(d).wait_send()
        rhs_copy(d).wait_send()
        props_copy(d).wait_send()
    for n in range(N_CHUNK):
        for part in range(3):
            core_copy(n, part).wait_send()
            for step in range(3):
                halving(n, part, step)[0].wait_send()

    def drain_tiles(d, carry):
        tile_copy(d).wait_send()
        spread_copy(d).wait_send()
        return carry

    lax.fori_loop(1, N_SAMPLE, drain_tiles, 0)


def store(inter_ref, props_ref, inter_out, props_out, sem):
    copies = (
        pltpu.make_async_copy(inter_ref, inter_out, sem.at[0]),
        pltpu.make_async_copy(props_ref, props_out, sem.at[1]),
    )
    for copy in copies:
        copy.start()
    for copy in copies:
        copy.wait()


def local(expression, profile, dosage, signature):
    s_dev, g_dev = expression.shape
    v_dev = dosage.shape[1]
    types = profile.shape[1]
    quarter, n_cols = s_dev // N_GENE, g_dev // N_CHUNK
    scale = 1.0 / math.sqrt(s_dev * N_SAMPLE)
    sig_cols = -(-signature.shape[0] // 128) * 128
    sizes = [hi - lo for lo, hi in PARTS]
    vmem, dma = pltpu.VMEM, pltpu.SemaphoreType.DMA
    inter, props_t = pl.pallas_call(
        functools.partial(kernel, scale),
        out_shape=(
            vmem((v_dev * types // N_SAMPLE, g_dev), F32),
            vmem((types, s_dev), F32),
        ),
        in_specs=[
            pl.BlockSpec(memory_space=pl.ANY),
            pl.BlockSpec(memory_space=pl.ANY),
            pl.BlockSpec(memory_space=pl.ANY),
            pl.BlockSpec(memory_space=pl.ANY),
        ],
        out_specs=(pl.BlockSpec(memory_space=pltpu.VMEM), pl.BlockSpec(memory_space=pltpu.VMEM)),
        scratch_shapes=[
            vmem((s_dev, g_dev), BF16),
            vmem((s_dev, v_dev), jnp.int32),
            vmem((v_dev, s_dev), BF16),
            vmem((v_dev * types + 16, s_dev), BF16),
            vmem((1, signature.shape[0]), jnp.int32),
            vmem((types, g_dev), F32),
            vmem((1, sig_cols), jnp.int32),
            vmem((8, g_dev), F32),
            [vmem((N_CHUNK, 2, 2, 2, k, 2, 8, n_cols), F32) for k in sizes],
            [vmem((N_CHUNK, 2, 2, 2, k, 8, n_cols), F32) for k in sizes],
            [vmem((N_CHUNK, 2, 2, k, 8, n_cols), F32) for k in sizes],
            [vmem((N_CHUNK, 2, k, 8, n_cols), F32) for k in sizes],
            [vmem((N_CHUNK, k, 8, n_cols), F32) for k in sizes],
            vmem((N_GENE, 8, quarter), F32),
            vmem((N_GENE, 8, quarter), F32),
            vmem((N_GENE - 1, 8, quarter), F32),
            vmem((8, 128), F32),
            vmem((N_GENE - 1, 8, 128), F32),
            vmem((v_dev, 128), F32),
            vmem((8, 128), F32),
            vmem((N_CHUNK, 8, n_cols), F32),
            vmem((3, 8, 128), F32),
            vmem((N_SAMPLE, 8, 128), F32),
            vmem((N_SAMPLE, 8, 128), F32),
            vmem((N_SAMPLE, 8, 128), F32),
            vmem((g_dev // 128, 8 * types, 128), F32),
            dma((N_GENE, 2)),
            dma((N_GENE,)),
            dma((2,)),
            dma,
            dma((N_GENE - 1,)),
            dma((N_GENE - 1,)),
            dma((N_GENE - 1,)),
            dma((N_CHUNK, 3)),
            dma((N_CHUNK, 3, 3)),
            dma,
            dma,
        ],
        compiler_params=pltpu.CompilerParams(
            collective_id=0, has_side_effects=True, vmem_limit_bytes=VMEM_BYTES
        ),
        name="eqtl",
    )(signature.reshape(1, -1), profile.T, expression, dosage)
    inter, props_t = pl.pallas_call(
        store,
        out_shape=(
            jax.ShapeDtypeStruct(inter.shape, F32),
            jax.ShapeDtypeStruct(props_t.shape, F32),
        ),
        in_specs=[pl.BlockSpec(memory_space=pltpu.VMEM)] * 2,
        out_specs=(pl.BlockSpec(memory_space=pl.ANY), pl.BlockSpec(memory_space=pl.ANY)),
        scratch_shapes=[dma((2,))],
        compiler_params=pltpu.CompilerParams(vmem_limit_bytes=8 * 1024 * 1024),
        name="store",
    )(inter, props_t)
    return inter, props_t.T


def solution(mesh):
    placed = (P("sample", "gene"), P("gene", None), P("sample", "variant"), P())
    return jax.shard_map(
        local,
        mesh=mesh,
        in_specs=placed,
        out_specs=(P(("variant", "sample"), "gene"), P("sample", None)),
        check_vma=False,
    )
```

```python
import functools
import math

import jax
import jax.numpy as jnp
from jax import lax
from jax.experimental import pallas as pl
from jax.experimental.pallas import tpu as pltpu
from jax.sharding import PartitionSpec as P

MESH = pl.DeviceIdType.MESH
HIGH = lax.Precision.HIGHEST
F32, BF16 = jnp.float32, jnp.bfloat16
NT = (((1,), (1,)), ((), ()))
N_GENE = 4
N_SAMPLE = 16
N_CHUNK = 4
VMEM_BYTES = 62_000_000
PARTS = ((0, 2), (2, 4), (4, 7))
ORDERS = (
    ("azb", "baz", "zba"),
    ("abz", "zba", "bza"),
    ("azb", "baz", "baz"),
    ("zab", "zba", "azb"),
)
AFTER = (
    (0, 2, 0), (3, 0, -1), (1, 0, 0), (3, 1, -1), (1, 1, 0), (3, 2, -1), (1, 2, 0), (0, 0, 1), (0, 1, 1), "spread",
    (2, 1, 0), (2, 0, 0), (3, 0, 0), (2, 2, 0), (3, 1, 0), (3, 2, 0), (0, 2, 1), (1, 2, 1), (1, 0, 1), (2, 1, 1),
    (1, 1, 1), (3, 0, 1), (2, 0, 1), (2, 2, 1), (3, 2, 1), (3, 1, 1),
)
LAST = (
    (0, 1), (0, 0), (1, 0), (0, 2), (2, 1), (1, 2), (3, 0), (1, 1), (2, 0), (2, 2), (3, 2), (3, 1),
)


def ldl(gram):
    row = lax.broadcasted_iota(jnp.int32, (8, 8), 0)
    col = lax.broadcasted_iota(jnp.int32, (8, 8), 1)
    eye = (row == col).astype(F32)
    a = jnp.where((row == 7) | (col == 7), eye, gram)
    inv, inv_t = eye, eye
    for j in range(6):
        piv = a[j : j + 1, j : j + 1]
        f_col = jnp.where(row[:, :1] > j, a[:, j : j + 1] / piv, 0.0)
        f_row = jnp.where(col[:1, :] > j, a[j : j + 1, :] / piv, 0.0)
        inv = inv - f_col * inv[j : j + 1, :]
        inv_t = inv_t - inv_t[:, j : j + 1] * f_row
        a = a - f_col * a[j : j + 1, :]
    diag = jnp.sum(a * eye, axis=1, keepdims=True)
    return inv, inv_t, diag


def solve(factor, rhs):
    inv, inv_t, diag = factor
    mid = inv[:, 0:1] * rhs[0:1, :]
    for j in range(1, 7):
        mid = mid + inv[:, j : j + 1] * rhs[j : j + 1, :]
    mid = mid / diag
    out = inv_t[:, 0:1] * mid[0:1, :]
    for j in range(1, 7):
        out = out + inv_t[:, j : j + 1] * mid[j : j + 1, :]
    return out


def kernel(
    scale,
    sig_hbm, prof_hbm, expr_hbm, dos_hbm,
    inter_ref, props_ref,
    e_v, d_v, d_t, des, sig_ref, prof_ref, sig_sc, m_sc, acc, rc, r1, r2, r3,
    pbuf, rsnd, rrcv, gsnd, grcv, corr_sc, pp_sc, py_sc, fac_sc, tsrc, trcv, tbuf, mix,
    e_sem, d_sem, i_sem, sent, g_r, x_r, p_r, c_r, h_r, t_r, u_r,
):
    s_dev, g_dev = e_v.shape
    quarter = s_dev // N_GENE
    half = quarter // 2
    n_cols = g_dev // N_CHUNK
    n_tiles = g_dev // 128
    per_chunk = n_cols // 128
    types = 7
    g = lax.axis_index("gene")
    s = lax.axis_index("sample")
    y, z, c = s // 4, (s // 2) % 2, s % 2
    b = y // 2
    a = (y + b) % 2
    place = {"a": a, "b": b, "z": z}
    other = {
        "a": (2 * b + (1 - a + b) % 2) * 4 + z * 2 + c,
        "b": (2 * (1 - b) + (a + 1 - b) % 2) * 4 + z * 2 + c,
        "z": s + 2 - 4 * z,
    }
    core = s + 1 - 2 * c

    def gene_of(d):
        return {"gene": (g + d) % N_GENE}

    def sample_of(d):
        return {"sample": (s + d) % N_SAMPLE}

    def quarter_of(d):
        return (g + N_GENE - d) % N_GENE

    def load(d, h):
        source = pl.ds(pl.multiple_of(quarter_of(d) * quarter + h * half, half), half)
        target = pl.ds(pl.multiple_of(d * quarter + h * half, half), half)
        return pltpu.make_async_copy(expr_hbm.at[source, :], e_v.at[target, :], e_sem.at[d, h])

    def load_dosage(d):
        source = pl.ds(pl.multiple_of(quarter_of(d) * quarter, quarter), quarter)
        return pltpu.make_async_copy(dos_hbm.at[source, :], d_v.at[pl.ds(d * quarter, quarter), :], d_sem.at[d])

    def remote(src, dst, recv, device):
        return pltpu.make_async_remote_copy(
            src_ref=src, dst_ref=dst, send_sem=sent, recv_sem=recv, device_id=device, device_id_type=MESH
        )

    sig_copy = pltpu.make_async_copy(sig_hbm, sig_ref, i_sem.at[0])
    prof_copy = pltpu.make_async_copy(prof_hbm, prof_ref, i_sem.at[1])
    sig_copy.start()
    prof_copy.start()
    for h in range(2):
        load(1, h).start()

    barrier = pltpu.get_barrier_semaphore()
    for d in range(1, N_GENE):
        pl.semaphore_signal(barrier, inc=1, device_id=gene_of(d), device_id_type=MESH)
    for d in range(1, N_SAMPLE):
        pl.semaphore_signal(barrier, inc=1, device_id=sample_of(d), device_id_type=MESH)

    n_sig = sig_ref.shape[1]
    sig_sc[...] = jnp.full(sig_sc.shape, -1, jnp.int32)
    sig_copy.wait()
    prof_copy.wait()
    for d in (2, 3, 0):
        for h in range(2):
            load(d, h).start()
    for d in range(N_GENE):
        load_dosage(d).start()
    sig_sc[0:1, 0:n_sig] = sig_ref[...]
    cols = []
    for t in range(sig_sc.shape[1] // 128):
        line = sig_sc[0:1, 128 * t : 128 * t + 128].astype(F32)
        cols.append(jnp.transpose(jnp.broadcast_to(line, (128, 128))))
    lane = lax.broadcasted_iota(jnp.int32, (128, 128), 1) + g * g_dev
    m_sc[...] = jnp.zeros(m_sc.shape, F32)
    for t in range(n_tiles):
        ids = (lane + 128 * t).astype(F32)
        hit = jnp.zeros((128, 128), F32)
        for column in cols:
            hit = jnp.where(column == ids, 1.0, hit)
        member = jnp.max(hit, axis=0, keepdims=True)
        m_sc[0:types, 128 * t : 128 * t + 128] = prof_ref[:, 128 * t : 128 * t + 128] * member
    masked = m_sc[...]
    gsnd[...] = jnp.zeros(gsnd.shape, F32)
    gsnd[:, 0:8] = lax.dot_general(masked, masked, NT, precision=HIGH, preferred_element_type=F32)
    top = masked.astype(BF16).astype(F32)
    rest = masked - top
    mid = rest.astype(BF16).astype(F32)
    m3 = jnp.concatenate([top, mid, rest - mid], axis=0).astype(BF16)

    def gram_copy(d):
        return remote(gsnd, grcv.at[d - 1], g_r.at[d - 1], gene_of(d))

    def rhs_copy(d):
        return remote(rsnd.at[d], rrcv.at[d - 1], x_r.at[d - 1], gene_of(d))

    def rhs_quarter(i, carry):
        d = N_GENE - 1 - i
        at = (N_GENE - d) % N_GENE
        for h in range(2):
            load(at, h).wait()
        for h in range(2):
            rows = pl.ds(pl.multiple_of(at * quarter + h * half, half), half)
            part = lax.dot_general(m3, e_v[rows, :], NT, preferred_element_type=F32)
            rsnd[d, :, h * half : (h + 1) * half] = part[0:8] + part[8:16] + part[16:24]

        @pl.when(i == 0)
        def _():
            pl.semaphore_wait(barrier, N_GENE - 1 + N_SAMPLE - 1)
            for peer in range(1, N_GENE):
                gram_copy(peer).start()

        @pl.when(d > 0)
        def _():
            rhs_copy(d).start()

        return carry

    lax.fori_loop(0, N_GENE, rhs_quarter, 0)

    for d in range(N_GENE):
        load_dosage(d).wait()
    for i in range(s_dev // 128):
        piece = d_v[128 * i : 128 * i + 128, :].astype(F32).astype(BF16)
        d_t[:, 128 * i : 128 * i + 128] = jnp.transpose(piece)
    corr_sc[...] = jnp.zeros(corr_sc.shape, F32)
    pp_sc[...] = jnp.zeros(pp_sc.shape, F32)
    gram = gsnd[:, 0:8]
    for d in range(1, N_GENE):
        gram_copy(d).wait_recv()
        gram = gram + grcv[d - 1, :, 0:8]
    factor = ldl(gram)
    for d in (3, 2, 1):
        rhs_copy(d).wait_recv()
    pbuf[g] = solve(factor, rsnd[0] + rrcv[2] + rrcv[1] + rrcv[0])

    def props_copy(d):
        return remote(pbuf.at[g], pbuf.at[g], p_r.at[d - 1], gene_of(d))

    for d in (2, 1, 3):
        props_copy(d).start()

    def span_of(d):
        return slice(d * quarter, (d + 1) * quarter)

    def design(d):
        props = pbuf[quarter_of(d)]
        props_ref[:, pl.ds(pl.multiple_of(quarter_of(d) * quarter, quarter), quarter)] = props[0:types]
        top = props.astype(BF16).astype(F32)
        des[896:912, span_of(d)] = jnp.concatenate([top, props - top], axis=0).astype(BF16)
        for k in range(types):
            lo, hi = [part for part in PARTS if part[0] <= k < part[1]][0]
            wide = jnp.broadcast_to(top[k : k + 1, :], (16, quarter)).astype(BF16)
            for bb in range(2):
                for aa in range(2):
                    for zz in range(2):
                        source = ((2 * bb + (aa + bb) % 2) * 2 + zz) * 16
                        target = lo * 128 + (((bb * 2 + aa) * 2 + zz) * (hi - lo) + k - lo) * 16
                        des[target : target + 16, span_of(d)] = d_t[source : source + 16, span_of(d)] * wide

    def small_term(d):
        span = pl.ds(pl.multiple_of(d * quarter, quarter), quarter)
        props = pbuf[quarter_of(d)]
        top = props.astype(BF16).astype(F32)
        highs, lows = [], []
        for k in range(types):
            weight = jnp.broadcast_to(top[k : k + 1, :], (8, quarter)) * props
            high = weight.astype(BF16).astype(F32)
            highs.append(high)
            lows.append(weight - high)
        w = jnp.concatenate(highs + lows, axis=0).astype(BF16)
        corr = lax.dot_general(d_t[:, span], w, NT, preferred_element_type=F32)
        both = des[896:912, span]
        pp = lax.dot_general(both, both, NT, preferred_element_type=F32)
        corr_sc[:, 0 : 16 * types] += corr
        pp_sc[:, 0:16] += pp[0:8] + pp[8:16]

    def term(n, first):
        columns = pl.ds(pl.multiple_of(n * n_cols, n_cols), n_cols)
        span = slice(0, quarter) if first else slice(quarter, s_dev)
        value = jnp.dot(des[:, span], e_v[span, columns], preferred_element_type=F32)
        for part, (lo, hi) in enumerate(PARTS):
            body = value[128 * lo : 128 * hi].reshape(acc[part].shape[1:])
            acc[part][n] = body if first else acc[part][n] + body
        tail = value[896:904] + value[904:912]
        py_sc[n] = tail if first else py_sc[n] + tail

    def core_copy(n, part):
        return remote(
            acc[part].at[n, :, :, :, :, 1 - c], rc[part].at[n], c_r.at[n, part], {"sample": core}
        )

    def halving(n, part, step):
        axes = ORDERS[n][part]
        kept = {axis: place[axis] for axis in axes[:step]}
        axis = axes[step]

        def block(fixed):
            return (n,) + tuple(fixed.get(name, slice(None)) for name in "baz") + (slice(None), c)

        landing = ((r1, r2, r3)[step])[part].at[n]
        copy = remote(
            acc[part].at[block({**kept, axis: 1 - place[axis]})],
            landing,
            h_r.at[n, part, step],
            {"sample": other[axis]},
        )
        return copy, block({**kept, axis: place[axis]}), landing

    def advance(n, part, step):
        if step < 0:
            core_copy(n, part).wait_recv()
            acc[part][n, :, :, :, :, c] += rc[part][n]
        else:
            copy, kept, landing = halving(n, part, step)
            copy.wait_recv()
            acc[part][kept] += landing[...]
        halving(n, part, step + 1)[0].start()

    def tile_copy(d):
        return remote(tsrc.at[(s + d) % N_SAMPLE], trcv.at[d], t_r, sample_of(d))

    def spread_copy(d):
        return remote(tbuf.at[0], tbuf.at[d], u_r, sample_of(d))

    def start_tiles(d, carry):
        tile_copy(d).start()
        return carry

    def wait_tiles(buffer, recv):
        remote(tsrc.at[1:N_SAMPLE], buffer.at[1:N_SAMPLE], recv, sample_of(1)).wait_recv()

    def start_spread(d, carry):
        spread_copy(d).start()
        return carry

    spot = lax.broadcasted_iota(jnp.int32, (8, 128), 1)
    n_kj = 8 * types

    def send_tiles():
        pp = pp_sc[...]
        pp = pltpu.roll(pp + pltpu.roll(pp, 120, 1), n_kj, 1)
        for i in range(N_SAMPLE):
            corr = corr_sc[8 * i : 8 * i + 8, :]
            corr = corr + pltpu.roll(corr, 128 - n_kj, 1)
            at = 64 * i
            py = py_sc[at // n_cols, :, at % n_cols // 128 * 128 : at % n_cols // 128 * 128 + 128]
            if i % 2 == 0:
                py = pltpu.roll(py, 64, 1)
            tsrc[i] = jnp.where(spot < n_kj, corr, jnp.where(spot < 64, pp, py))
        lax.fori_loop(1, N_SAMPLE, start_tiles, 0)

    def spread_tiles():
        wait_tiles(trcv, t_r)
        total = tsrc[s]
        for d in range(1, N_SAMPLE):
            total = total + trcv[d]
        tbuf[0] = total
        lax.fori_loop(1, N_SAMPLE, start_spread, 0)
        corr_sc[0:8, :] = total
        inv, inv_t, diag = ldl(pltpu.roll(total, 128 - n_kj, 1)[:, 0:8])
        fac_sc[0, :, 0:8] = inv
        fac_sc[1, :, 0:8] = inv_t
        fac_sc[2, :, 0:1] = diag

    def solve_coef():
        wait_tiles(tbuf, u_r)
        factor = fac_sc[0, :, 0:8], fac_sc[1, :, 0:8], fac_sc[2, :, 0:1]
        own = [tbuf[(s + N_SAMPLE - i) % N_SAMPLE] for i in range(N_SAMPLE)]
        tiles = [jnp.where(spot < 64, pltpu.roll(own[2 * i], 64, 1), own[2 * i + 1]) for i in range(n_tiles)]
        m_sc[...] = solve(factor, jnp.concatenate(tiles, axis=1))

    def finish(n, part):
        corr = corr_sc[0:8, :]
        coef = m_sc[:, n * n_cols : (n + 1) * n_cols]
        copy, kept, landing = halving(n, part, 2)
        copy.wait_recv()
        value = acc[part][kept] + landing[...]
        for k in range(*PARTS[part]):
            out = value[k - PARTS[part][0]]
            for j in range(types):
                out = out - corr[:, 8 * k + j : 8 * k + j + 1] * coef[j : j + 1, :]
            out = out * scale
            for i in range(per_chunk):
                mix[n * per_chunk + i, pl.ds(k, 8, stride=types), :] = out[:, 128 * i : 128 * i + 128]

    design(0)

    def own(n, carry):
        term(n, True)
        return carry

    lax.fori_loop(0, N_CHUNK, own, 0)
    small_term(0)
    for d in (1, 3, 2):
        props_copy(d).wait_recv()
        design(d)

    def others(n, carry):
        term(n, False)
        for part in range(3):
            core_copy(n, part).start()

        @pl.when(n > 0)
        def _():
            small_term(n)

        @pl.when(n == N_CHUNK - 1)
        def _():
            send_tiles()

        for chunk in range(1, N_CHUNK):
            @pl.when(n == chunk)
            def _(chunk=chunk):
                if chunk == N_CHUNK - 1:
                    advance(0, 0, 0)
                    advance(0, 1, 0)
                for part in range(3):
                    advance(chunk - 1, part, -1)

        return carry

    lax.fori_loop(0, N_CHUNK, others, 0)
    for event in AFTER:
        if event == "spread":
            spread_tiles()
        else:
            advance(*event)
    solve_coef()
    left = [3] * N_CHUNK
    for n, part in LAST:
        finish(n, part)
        left[n] -= 1
        if left[n] == 0:
            for i in range(n * per_chunk, (n + 1) * per_chunk):
                inter_ref[:, 128 * i : 128 * i + 128] = mix[i]

    for d in range(1, N_GENE):
        gram_copy(d).wait_send()
        rhs_copy(d).wait_send()
        props_copy(d).wait_send()
    for n in range(N_CHUNK):
        for part in range(3):
            core_copy(n, part).wait_send()
            for step in range(3):
                halving(n, part, step)[0].wait_send()

    def drain_tiles(d, carry):
        tile_copy(d).wait_send()
        spread_copy(d).wait_send()
        return carry

    lax.fori_loop(1, N_SAMPLE, drain_tiles, 0)


def store(inter_ref, props_ref, inter_out, props_out, sem):
    copies = (
        pltpu.make_async_copy(inter_ref, inter_out, sem.at[0]),
        pltpu.make_async_copy(props_ref, props_out, sem.at[1]),
    )
    for copy in copies:
        copy.start()
    for copy in copies:
        copy.wait()


def local(expression, profile, dosage, signature):
    s_dev, g_dev = expression.shape
    v_dev = dosage.shape[1]
    types = profile.shape[1]
    quarter, n_cols = s_dev // N_GENE, g_dev // N_CHUNK
    scale = 1.0 / math.sqrt(s_dev * N_SAMPLE)
    sig_cols = -(-signature.shape[0] // 128) * 128
    sizes = [hi - lo for lo, hi in PARTS]
    vmem, dma = pltpu.VMEM, pltpu.SemaphoreType.DMA
    inter, props_t = pl.pallas_call(
        functools.partial(kernel, scale),
        out_shape=(
            vmem((v_dev * types // N_SAMPLE, g_dev), F32),
            vmem((types, s_dev), F32),
        ),
        in_specs=[
            pl.BlockSpec(memory_space=pl.ANY),
            pl.BlockSpec(memory_space=pl.ANY),
            pl.BlockSpec(memory_space=pl.ANY),
            pl.BlockSpec(memory_space=pl.ANY),
        ],
        out_specs=(pl.BlockSpec(memory_space=pltpu.VMEM), pl.BlockSpec(memory_space=pltpu.VMEM)),
        scratch_shapes=[
            vmem((s_dev, g_dev), BF16),
            vmem((s_dev, v_dev), jnp.int32),
            vmem((v_dev, s_dev), BF16),
            vmem((v_dev * types + 16, s_dev), BF16),
            vmem((1, signature.shape[0]), jnp.int32),
            vmem((types, g_dev), F32),
            vmem((1, sig_cols), jnp.int32),
            vmem((8, g_dev), F32),
            [vmem((N_CHUNK, 2, 2, 2, k, 2, 8, n_cols), F32) for k in sizes],
            [vmem((N_CHUNK, 2, 2, 2, k, 8, n_cols), F32) for k in sizes],
            [vmem((N_CHUNK, 2, 2, k, 8, n_cols), F32) for k in sizes],
            [vmem((N_CHUNK, 2, k, 8, n_cols), F32) for k in sizes],
            [vmem((N_CHUNK, k, 8, n_cols), F32) for k in sizes],
            vmem((N_GENE, 8, quarter), F32),
            vmem((N_GENE, 8, quarter), F32),
            vmem((N_GENE - 1, 8, quarter), F32),
            vmem((8, 128), F32),
            vmem((N_GENE - 1, 8, 128), F32),
            vmem((v_dev, 128), F32),
            vmem((8, 128), F32),
            vmem((N_CHUNK, 8, n_cols), F32),
            vmem((3, 8, 128), F32),
            vmem((N_SAMPLE, 8, 128), F32),
            vmem((N_SAMPLE, 8, 128), F32),
            vmem((N_SAMPLE, 8, 128), F32),
            vmem((g_dev // 128, 8 * types, 128), F32),
            dma((N_GENE, 2)),
            dma((N_GENE,)),
            dma((2,)),
            dma,
            dma((N_GENE - 1,)),
            dma((N_GENE - 1,)),
            dma((N_GENE - 1,)),
            dma((N_CHUNK, 3)),
            dma((N_CHUNK, 3, 3)),
            dma,
            dma,
        ],
        compiler_params=pltpu.CompilerParams(
            collective_id=0, has_side_effects=True, vmem_limit_bytes=VMEM_BYTES
        ),
        name="eqtl",
    )(signature.reshape(1, -1), profile.T, expression, dosage)
    inter, props_t = pl.pallas_call(
        store,
        out_shape=(
            jax.ShapeDtypeStruct(inter.shape, F32),
            jax.ShapeDtypeStruct(props_t.shape, F32),
        ),
        in_specs=[pl.BlockSpec(memory_space=pltpu.VMEM)] * 2,
        out_specs=(pl.BlockSpec(memory_space=pl.ANY), pl.BlockSpec(memory_space=pl.ANY)),
        scratch_shapes=[dma((2,))],
        compiler_params=pltpu.CompilerParams(vmem_limit_bytes=8 * 1024 * 1024),
        name="store",
    )(inter, props_t)
    return inter, props_t.T


def solution(mesh):
    placed = (P("sample", "gene"), P("gene", None), P("sample", "variant"), P())
    return jax.shard_map(
        local,
        mesh=mesh,
        in_specs=placed,
        out_specs=(P(("variant", "sample"), "gene"), P("sample", None)),
        check_vma=False,
    )
```

```python
import functools
import math

import jax
import jax.numpy as jnp
from jax import lax
from jax.experimental import pallas as pl
from jax.experimental.pallas import tpu as pltpu
from jax.sharding import PartitionSpec as P

MESH = pl.DeviceIdType.MESH
HIGH = lax.Precision.HIGHEST
F32, BF16 = jnp.float32, jnp.bfloat16
NT = (((1,), (1,)), ((), ()))
N_GENE = 4
N_SAMPLE = 16
N_CHUNK = 4
VMEM_BYTES = 62_000_000
PARTS = ((0, 2), (2, 4), (4, 7))
ORDERS = (
    ("azb", "baz", "zba"),
    ("abz", "zba", "bza"),
    ("azb", "baz", "baz"),
    ("zab", "zba", "azb"),
)
AFTER = (
    (0, 2, 0), "small", (3, 0, -1), (1, 0, 0), (3, 1, -1), (1, 1, 0), (3, 2, -1), (1, 2, 0), (0, 0, 1), (0, 1, 1), "spread",
    (2, 1, 0), (2, 0, 0), (3, 0, 0), (2, 2, 0), (3, 1, 0), (3, 2, 0), (0, 2, 1), (1, 2, 1), (1, 0, 1), (2, 1, 1),
    (1, 1, 1), (3, 0, 1), (2, 0, 1), (2, 2, 1), (3, 2, 1), (3, 1, 1),
)
LAST = (
    (0, 1), (0, 0), (1, 0), (0, 2), (2, 1), (1, 2), (3, 0), (1, 1), (2, 0), (2, 2), (3, 2), (3, 1),
)


def ldl(gram):
    row = lax.broadcasted_iota(jnp.int32, (8, 8), 0)
    col = lax.broadcasted_iota(jnp.int32, (8, 8), 1)
    eye = (row == col).astype(F32)
    a = jnp.where((row == 7) | (col == 7), eye, gram)
    inv, inv_t = eye, eye
    for j in range(6):
        piv = a[j : j + 1, j : j + 1]
        f_col = jnp.where(row[:, :1] > j, a[:, j : j + 1] / piv, 0.0)
        f_row = jnp.where(col[:1, :] > j, a[j : j + 1, :] / piv, 0.0)
        inv = inv - f_col * inv[j : j + 1, :]
        inv_t = inv_t - inv_t[:, j : j + 1] * f_row
        a = a - f_col * a[j : j + 1, :]
    diag = jnp.sum(a * eye, axis=1, keepdims=True)
    return inv, inv_t, diag


def solve(factor, rhs):
    inv, inv_t, diag = factor
    mid = inv[:, 0:1] * rhs[0:1, :]
    for j in range(1, 7):
        mid = mid + inv[:, j : j + 1] * rhs[j : j + 1, :]
    mid = mid / diag
    out = inv_t[:, 0:1] * mid[0:1, :]
    for j in range(1, 7):
        out = out + inv_t[:, j : j + 1] * mid[j : j + 1, :]
    return out


def kernel(
    scale,
    sig_hbm, prof_hbm, expr_hbm, dos_hbm,
    inter_ref, props_ref,
    e_v, d_v, d_t, des, sig_ref, prof_ref, sig_sc, m_sc, acc, rc, r1, r2, r3,
    pbuf, rsnd, rrcv, gsnd, grcv, corr_sc, pp_sc, py_sc, fac_sc, tsrc, trcv, tbuf, mix,
    e_sem, d_sem, i_sem, sent, g_r, x_r, p_r, c_r, h_r, t_r, u_r,
):
    s_dev, g_dev = e_v.shape
    quarter = s_dev // N_GENE
    half = quarter // 2
    n_cols = g_dev // N_CHUNK
    n_tiles = g_dev // 128
    per_chunk = n_cols // 128
    types = 7
    g = lax.axis_index("gene")
    s = lax.axis_index("sample")
    y, z, c = s // 4, (s // 2) % 2, s % 2
    b = y // 2
    a = (y + b) % 2
    place = {"a": a, "b": b, "z": z}
    other = {
        "a": (2 * b + (1 - a + b) % 2) * 4 + z * 2 + c,
        "b": (2 * (1 - b) + (a + 1 - b) % 2) * 4 + z * 2 + c,
        "z": s + 2 - 4 * z,
    }
    core = s + 1 - 2 * c

    def gene_of(d):
        return {"gene": (g + d) % N_GENE}

    def sample_of(d):
        return {"sample": (s + d) % N_SAMPLE}

    def quarter_of(d):
        return (g + N_GENE - d) % N_GENE

    def load(d, h):
        source = pl.ds(pl.multiple_of(quarter_of(d) * quarter + h * half, half), half)
        target = pl.ds(pl.multiple_of(d * quarter + h * half, half), half)
        return pltpu.make_async_copy(expr_hbm.at[source, :], e_v.at[target, :], e_sem.at[d, h])

    def load_dosage(d):
        source = pl.ds(pl.multiple_of(quarter_of(d) * quarter, quarter), quarter)
        return pltpu.make_async_copy(dos_hbm.at[source, :], d_v.at[pl.ds(d * quarter, quarter), :], d_sem.at[d])

    def remote(src, dst, recv, device):
        return pltpu.make_async_remote_copy(
            src_ref=src, dst_ref=dst, send_sem=sent, recv_sem=recv, device_id=device, device_id_type=MESH
        )

    sig_copy = pltpu.make_async_copy(sig_hbm, sig_ref, i_sem.at[0])
    prof_copy = pltpu.make_async_copy(prof_hbm, prof_ref, i_sem.at[1])
    sig_copy.start()
    prof_copy.start()
    barrier = pltpu.get_barrier_semaphore()
    for d in range(1, N_GENE):
        pl.semaphore_signal(barrier, inc=1, device_id=gene_of(d), device_id_type=MESH)
    for d in range(1, N_SAMPLE):
        pl.semaphore_signal(barrier, inc=1, device_id=sample_of(d), device_id_type=MESH)

    for h in range(2):
        load(1, h).start()

    n_sig = sig_ref.shape[1]
    sig_sc[...] = jnp.full(sig_sc.shape, -1, jnp.int32)
    sig_copy.wait()
    prof_copy.wait()
    for d in (2, 3, 0):
        for h in range(2):
            load(d, h).start()
    for d in range(N_GENE):
        load_dosage(d).start()
    sig_sc[0:1, 0:n_sig] = sig_ref[...]
    cols = []
    for t in range(sig_sc.shape[1] // 128):
        line = sig_sc[0:1, 128 * t : 128 * t + 128].astype(F32)
        cols.append(jnp.transpose(jnp.broadcast_to(line, (128, 128))))
    lane = lax.broadcasted_iota(jnp.int32, (128, 128), 1) + g * g_dev
    m_sc[...] = jnp.zeros(m_sc.shape, F32)
    for t in range(n_tiles):
        ids = (lane + 128 * t).astype(F32)
        hit = jnp.zeros((128, 128), F32)
        for column in cols:
            hit = jnp.where(column == ids, 1.0, hit)
        member = jnp.max(hit, axis=0, keepdims=True)
        m_sc[0:types, 128 * t : 128 * t + 128] = prof_ref[:, 128 * t : 128 * t + 128] * member
    masked = m_sc[...]
    gsnd[...] = jnp.zeros(gsnd.shape, F32)
    gsnd[:, 0:8] = lax.dot_general(masked, masked, NT, precision=HIGH, preferred_element_type=F32)
    top = masked.astype(BF16).astype(F32)
    rest = masked - top
    mid = rest.astype(BF16).astype(F32)
    m3 = jnp.concatenate([top, mid, rest - mid], axis=0).astype(BF16)

    def gram_copy(d):
        return remote(gsnd, grcv.at[d - 1], g_r.at[d - 1], gene_of(d))

    def rhs_copy(d):
        return remote(rsnd.at[d], rrcv.at[d - 1], x_r.at[d - 1], gene_of(d))

    def rhs_quarter(i, carry):
        d = N_GENE - 1 - i
        at = (N_GENE - d) % N_GENE
        for h in range(2):
            load(at, h).wait()
        for h in range(2):
            rows = pl.ds(pl.multiple_of(at * quarter + h * half, half), half)
            part = lax.dot_general(m3, e_v[rows, :], NT, preferred_element_type=F32)
            rsnd[d, :, h * half : (h + 1) * half] = part[0:8] + part[8:16] + part[16:24]

        @pl.when(i == 0)
        def _():
            pl.semaphore_wait(barrier, N_GENE - 1 + N_SAMPLE - 1)
            for peer in range(1, N_GENE):
                gram_copy(peer).start()

        @pl.when(d > 0)
        def _():
            rhs_copy(d).start()

        return carry

    lax.fori_loop(0, N_GENE, rhs_quarter, 0)

    for d in range(N_GENE):
        load_dosage(d).wait()
    for i in range(s_dev // 128):
        piece = d_v[128 * i : 128 * i + 128, :].astype(F32).astype(BF16)
        d_t[:, 128 * i : 128 * i + 128] = jnp.transpose(piece)
    corr_sc[...] = jnp.zeros(corr_sc.shape, F32)
    pp_sc[...] = jnp.zeros(pp_sc.shape, F32)
    gram = gsnd[:, 0:8]
    for d in range(1, N_GENE):
        gram_copy(d).wait_recv()
        gram = gram + grcv[d - 1, :, 0:8]
    factor = ldl(gram)
    for d in (3, 2, 1):
        rhs_copy(d).wait_recv()
    pbuf[g] = solve(factor, rsnd[0] + rrcv[2] + rrcv[1] + rrcv[0])

    def props_copy(d):
        return remote(pbuf.at[g], pbuf.at[g], p_r.at[d - 1], gene_of(d))

    for d in (2, 1, 3):
        props_copy(d).start()

    def span_of(d):
        return slice(d * quarter, (d + 1) * quarter)

    def design(d):
        props = pbuf[quarter_of(d)]
        props_ref[:, pl.ds(pl.multiple_of(quarter_of(d) * quarter, quarter), quarter)] = props[0:types]
        top = props.astype(BF16).astype(F32)
        des[896:912, span_of(d)] = jnp.concatenate([top, props - top], axis=0).astype(BF16)
        for k in range(types):
            lo, hi = [part for part in PARTS if part[0] <= k < part[1]][0]
            wide = jnp.broadcast_to(top[k : k + 1, :], (16, quarter)).astype(BF16)
            for bb in range(2):
                for aa in range(2):
                    for zz in range(2):
                        source = ((2 * bb + (aa + bb) % 2) * 2 + zz) * 16
                        target = lo * 128 + (((bb * 2 + aa) * 2 + zz) * (hi - lo) + k - lo) * 16
                        des[target : target + 16, span_of(d)] = d_t[source : source + 16, span_of(d)] * wide

    def small_term(d):
        span = pl.ds(pl.multiple_of(d * quarter, quarter), quarter)
        props = pbuf[quarter_of(d)]
        top = props.astype(BF16).astype(F32)
        highs, lows = [], []
        for k in range(types):
            weight = jnp.broadcast_to(top[k : k + 1, :], (8, quarter)) * props
            high = weight.astype(BF16).astype(F32)
            highs.append(high)
            lows.append(weight - high)
        w = jnp.concatenate(highs + lows, axis=0).astype(BF16)
        corr = lax.dot_general(d_t[:, span], w, NT, preferred_element_type=F32)
        both = des[896:912, span]
        pp = lax.dot_general(both, both, NT, preferred_element_type=F32)
        corr_sc[:, 0 : 16 * types] += corr
        pp_sc[:, 0:16] += pp[0:8] + pp[8:16]

    def term(n, first):
        columns = pl.ds(pl.multiple_of(n * n_cols, n_cols), n_cols)
        span = slice(0, quarter) if first else slice(quarter, s_dev)
        value = jnp.dot(des[:, span], e_v[span, columns], preferred_element_type=F32)
        for part, (lo, hi) in enumerate(PARTS):
            body = value[128 * lo : 128 * hi].reshape(acc[part].shape[1:])
            acc[part][n] = body if first else acc[part][n] + body
        tail = value[896:904] + value[904:912]
        py_sc[n] = tail if first else py_sc[n] + tail

    def core_copy(n, part):
        return remote(
            acc[part].at[n, :, :, :, :, 1 - c], rc[part].at[n], c_r.at[n, part], {"sample": core}
        )

    def halving(n, part, step):
        axes = ORDERS[n][part]
        kept = {axis: place[axis] for axis in axes[:step]}
        axis = axes[step]

        def block(fixed):
            return (n,) + tuple(fixed.get(name, slice(None)) for name in "baz") + (slice(None), c)

        landing = ((r1, r2, r3)[step])[part].at[n]
        copy = remote(
            acc[part].at[block({**kept, axis: 1 - place[axis]})],
            landing,
            h_r.at[n, part, step],
            {"sample": other[axis]},
        )
        return copy, block({**kept, axis: place[axis]}), landing

    def advance(n, part, step):
        if step < 0:
            core_copy(n, part).wait_recv()
            acc[part][n, :, :, :, :, c] += rc[part][n]
        else:
            copy, kept, landing = halving(n, part, step)
            copy.wait_recv()
            acc[part][kept] += landing[...]
        halving(n, part, step + 1)[0].start()

    def tile_copy(d):
        return remote(tsrc.at[(s + d) % N_SAMPLE], trcv.at[d], t_r, sample_of(d))

    def spread_copy(d):
        return remote(tbuf.at[0], tbuf.at[d], u_r, sample_of(d))

    def start_tiles(d, carry):
        tile_copy(d).start()
        return carry

    def wait_tiles(buffer, recv):
        remote(tsrc.at[1:N_SAMPLE], buffer.at[1:N_SAMPLE], recv, sample_of(1)).wait_recv()

    def start_spread(d, carry):
        spread_copy(d).start()
        return carry

    spot = lax.broadcasted_iota(jnp.int32, (8, 128), 1)
    n_kj = 8 * types

    def send_tiles():
        pp = pp_sc[...]
        pp = pltpu.roll(pp + pltpu.roll(pp, 120, 1), n_kj, 1)
        for i in range(N_SAMPLE):
            corr = corr_sc[8 * i : 8 * i + 8, :]
            corr = corr + pltpu.roll(corr, 128 - n_kj, 1)
            at = 64 * i
            py = py_sc[at // n_cols, :, at % n_cols // 128 * 128 : at % n_cols // 128 * 128 + 128]
            if i % 2 == 0:
                py = pltpu.roll(py, 64, 1)
            tsrc[i] = jnp.where(spot < n_kj, corr, jnp.where(spot < 64, pp, py))
        lax.fori_loop(1, N_SAMPLE, start_tiles, 0)

    def spread_tiles():
        wait_tiles(trcv, t_r)
        total = tsrc[s]
        for d in range(1, N_SAMPLE):
            total = total + trcv[d]
        tbuf[0] = total
        lax.fori_loop(1, N_SAMPLE, start_spread, 0)
        corr_sc[0:8, :] = total
        inv, inv_t, diag = ldl(pltpu.roll(total, 128 - n_kj, 1)[:, 0:8])
        fac_sc[0, :, 0:8] = inv
        fac_sc[1, :, 0:8] = inv_t
        fac_sc[2, :, 0:1] = diag

    def solve_coef():
        wait_tiles(tbuf, u_r)
        factor = fac_sc[0, :, 0:8], fac_sc[1, :, 0:8], fac_sc[2, :, 0:1]
        own = [tbuf[(s + N_SAMPLE - i) % N_SAMPLE] for i in range(N_SAMPLE)]
        tiles = [jnp.where(spot < 64, pltpu.roll(own[2 * i], 64, 1), own[2 * i + 1]) for i in range(n_tiles)]
        m_sc[...] = solve(factor, jnp.concatenate(tiles, axis=1))

    def finish(n, part):
        corr = corr_sc[0:8, :]
        coef = m_sc[:, n * n_cols : (n + 1) * n_cols]
        copy, kept, landing = halving(n, part, 2)
        copy.wait_recv()
        value = acc[part][kept] + landing[...]
        for k in range(*PARTS[part]):
            out = value[k - PARTS[part][0]]
            for j in range(types):
                out = out - corr[:, 8 * k + j : 8 * k + j + 1] * coef[j : j + 1, :]
            out = out * scale
            for i in range(per_chunk):
                mix[n * per_chunk + i, pl.ds(k, 8, stride=types), :] = out[:, 128 * i : 128 * i + 128]

    design(0)

    def own(n, carry):
        term(n, True)
        return carry

    lax.fori_loop(0, N_CHUNK, own, 0)
    small_term(0)
    for d in (1, 3, 2):
        props_copy(d).wait_recv()
        design(d)

    def others(n, carry):
        term(n, False)
        for part in range(3):
            core_copy(n, part).start()

        for chunk in range(1, N_CHUNK):
            @pl.when(n == chunk)
            def _(chunk=chunk):
                if chunk == N_CHUNK - 1:
                    advance(0, 0, 0)
                    advance(0, 1, 0)
                for part in range(3):
                    advance(chunk - 1, part, -1)

        return carry

    lax.fori_loop(0, N_CHUNK, others, 0)

    def small_more(d, carry):
        small_term(d)
        return carry

    for event in AFTER:
        if event == "small":
            lax.fori_loop(1, N_GENE, small_more, 0)
            send_tiles()
        elif event == "spread":
            spread_tiles()
        else:
            advance(*event)
    solve_coef()
    left = [3] * N_CHUNK
    for n, part in LAST:
        finish(n, part)
        left[n] -= 1
        if left[n] == 0:
            for i in range(n * per_chunk, (n + 1) * per_chunk):
                inter_ref[:, 128 * i : 128 * i + 128] = mix[i]

    for d in range(1, N_GENE):
        gram_copy(d).wait_send()
        rhs_copy(d).wait_send()
        props_copy(d).wait_send()
    for n in range(N_CHUNK):
        for part in range(3):
            core_copy(n, part).wait_send()
            for step in range(3):
                halving(n, part, step)[0].wait_send()

    def drain_tiles(d, carry):
        tile_copy(d).wait_send()
        spread_copy(d).wait_send()
        return carry

    lax.fori_loop(1, N_SAMPLE, drain_tiles, 0)


def store(inter_ref, props_ref, inter_out, props_out, sem):
    copies = (
        pltpu.make_async_copy(inter_ref, inter_out, sem.at[0]),
        pltpu.make_async_copy(props_ref, props_out, sem.at[1]),
    )
    for copy in copies:
        copy.start()
    for copy in copies:
        copy.wait()


def local(expression, profile, dosage, signature):
    s_dev, g_dev = expression.shape
    v_dev = dosage.shape[1]
    types = profile.shape[1]
    quarter, n_cols = s_dev // N_GENE, g_dev // N_CHUNK
    scale = 1.0 / math.sqrt(s_dev * N_SAMPLE)
    sig_cols = -(-signature.shape[0] // 128) * 128
    sizes = [hi - lo for lo, hi in PARTS]
    vmem, dma = pltpu.VMEM, pltpu.SemaphoreType.DMA
    inter, props_t = pl.pallas_call(
        functools.partial(kernel, scale),
        out_shape=(
            vmem((v_dev * types // N_SAMPLE, g_dev), F32),
            vmem((types, s_dev), F32),
        ),
        in_specs=[
            pl.BlockSpec(memory_space=pl.ANY),
            pl.BlockSpec(memory_space=pl.ANY),
            pl.BlockSpec(memory_space=pl.ANY),
            pl.BlockSpec(memory_space=pl.ANY),
        ],
        out_specs=(pl.BlockSpec(memory_space=pltpu.VMEM), pl.BlockSpec(memory_space=pltpu.VMEM)),
        scratch_shapes=[
            vmem((s_dev, g_dev), BF16),
            vmem((s_dev, v_dev), jnp.int32),
            vmem((v_dev, s_dev), BF16),
            vmem((v_dev * types + 16, s_dev), BF16),
            vmem((1, signature.shape[0]), jnp.int32),
            vmem((types, g_dev), F32),
            vmem((1, sig_cols), jnp.int32),
            vmem((8, g_dev), F32),
            [vmem((N_CHUNK, 2, 2, 2, k, 2, 8, n_cols), F32) for k in sizes],
            [vmem((N_CHUNK, 2, 2, 2, k, 8, n_cols), F32) for k in sizes],
            [vmem((N_CHUNK, 2, 2, k, 8, n_cols), F32) for k in sizes],
            [vmem((N_CHUNK, 2, k, 8, n_cols), F32) for k in sizes],
            [vmem((N_CHUNK, k, 8, n_cols), F32) for k in sizes],
            vmem((N_GENE, 8, quarter), F32),
            vmem((N_GENE, 8, quarter), F32),
            vmem((N_GENE - 1, 8, quarter), F32),
            vmem((8, 128), F32),
            vmem((N_GENE - 1, 8, 128), F32),
            vmem((v_dev, 128), F32),
            vmem((8, 128), F32),
            vmem((N_CHUNK, 8, n_cols), F32),
            vmem((3, 8, 128), F32),
            vmem((N_SAMPLE, 8, 128), F32),
            vmem((N_SAMPLE, 8, 128), F32),
            vmem((N_SAMPLE, 8, 128), F32),
            vmem((g_dev // 128, 8 * types, 128), F32),
            dma((N_GENE, 2)),
            dma((N_GENE,)),
            dma((2,)),
            dma,
            dma((N_GENE - 1,)),
            dma((N_GENE - 1,)),
            dma((N_GENE - 1,)),
            dma((N_CHUNK, 3)),
            dma((N_CHUNK, 3, 3)),
            dma,
            dma,
        ],
        compiler_params=pltpu.CompilerParams(
            collective_id=0, has_side_effects=True, vmem_limit_bytes=VMEM_BYTES
        ),
        name="eqtl",
    )(signature.reshape(1, -1), profile.T, expression, dosage)
    inter, props_t = pl.pallas_call(
        store,
        out_shape=(
            jax.ShapeDtypeStruct(inter.shape, F32),
            jax.ShapeDtypeStruct(props_t.shape, F32),
        ),
        in_specs=[pl.BlockSpec(memory_space=pltpu.VMEM)] * 2,
        out_specs=(pl.BlockSpec(memory_space=pl.ANY), pl.BlockSpec(memory_space=pl.ANY)),
        scratch_shapes=[dma((2,))],
        compiler_params=pltpu.CompilerParams(vmem_limit_bytes=8 * 1024 * 1024),
        name="store",
    )(inter, props_t)
    return inter, props_t.T


def solution(mesh):
    placed = (P("sample", "gene"), P("gene", None), P("sample", "variant"), P())
    return jax.shard_map(
        local,
        mesh=mesh,
        in_specs=placed,
        out_specs=(P(("variant", "sample"), "gene"), P("sample", None)),
        check_vma=False,
    )
```

```python
import functools
import math

import jax
import jax.numpy as jnp
from jax import lax
from jax.experimental import pallas as pl
from jax.experimental.pallas import tpu as pltpu
from jax.sharding import PartitionSpec as P

MESH = pl.DeviceIdType.MESH
HIGH = lax.Precision.HIGHEST
F32, BF16 = jnp.float32, jnp.bfloat16
NT = (((1,), (1,)), ((), ()))
N_GENE = 4
N_SAMPLE = 16
N_CHUNK = 4
VMEM_BYTES = 62_000_000
PARTS = ((0, 2), (2, 4), (4, 7))
ORDERS = (
    ("azb", "baz", "zba"),
    ("abz", "zba", "bza"),
    ("azb", "baz", "baz"),
    ("zab", "zba", "azb"),
)
AFTER = (
    (0, 2, 0), (3, 0, -1), (1, 0, 0), (3, 1, -1), (1, 1, 0), (3, 2, -1), (1, 2, 0), (0, 0, 1), (0, 1, 1), "spread",
    (2, 1, 0), (2, 0, 0), (3, 0, 0), "factor", (2, 2, 0), (3, 1, 0), (3, 2, 0), (0, 2, 1), (1, 2, 1), (1, 0, 1), (2, 1, 1),
    (1, 1, 1), (3, 0, 1), (2, 0, 1), (2, 2, 1), (3, 2, 1), (3, 1, 1),
)
LAST = (
    (0, 1), (0, 0), (1, 0), (0, 2), (2, 1), (1, 2), (3, 0), (1, 1), (2, 0), (2, 2), (3, 2), (3, 1),
)


def ldl(gram):
    row = lax.broadcasted_iota(jnp.int32, (8, 8), 0)
    col = lax.broadcasted_iota(jnp.int32, (8, 8), 1)
    eye = (row == col).astype(F32)
    a = jnp.where((row == 7) | (col == 7), eye, gram)
    inv, inv_t = eye, eye
    for j in range(6):
        piv = a[j : j + 1, j : j + 1]
        f_col = jnp.where(row[:, :1] > j, a[:, j : j + 1] / piv, 0.0)
        f_row = jnp.where(col[:1, :] > j, a[j : j + 1, :] / piv, 0.0)
        inv = inv - f_col * inv[j : j + 1, :]
        inv_t = inv_t - inv_t[:, j : j + 1] * f_row
        a = a - f_col * a[j : j + 1, :]
    diag = jnp.sum(a * eye, axis=1, keepdims=True)
    return inv, inv_t, diag


def solve(factor, rhs):
    inv, inv_t, diag = factor
    mid = inv[:, 0:1] * rhs[0:1, :]
    for j in range(1, 7):
        mid = mid + inv[:, j : j + 1] * rhs[j : j + 1, :]
    mid = mid / diag
    out = inv_t[:, 0:1] * mid[0:1, :]
    for j in range(1, 7):
        out = out + inv_t[:, j : j + 1] * mid[j : j + 1, :]
    return out


def kernel(
    scale,
    sig_hbm, prof_hbm, expr_hbm, dos_hbm,
    inter_ref, props_ref,
    e_v, d_v, d_t, des, sig_ref, prof_ref, sig_sc, m_sc, acc, rc, r1, r2, r3,
    pbuf, rsnd, rrcv, gsnd, grcv, corr_sc, pp_sc, py_sc, fac_sc, tsrc, trcv, tbuf, mix,
    e_sem, d_sem, i_sem, sent, g_r, x_r, p_r, c_r, h_r, t_r, u_r,
):
    s_dev, g_dev = e_v.shape
    quarter = s_dev // N_GENE
    half = quarter // 2
    n_cols = g_dev // N_CHUNK
    n_tiles = g_dev // 128
    per_chunk = n_cols // 128
    types = 7
    g = lax.axis_index("gene")
    s = lax.axis_index("sample")
    y, z, c = s // 4, (s // 2) % 2, s % 2
    b = y // 2
    a = (y + b) % 2
    place = {"a": a, "b": b, "z": z}
    other = {
        "a": (2 * b + (1 - a + b) % 2) * 4 + z * 2 + c,
        "b": (2 * (1 - b) + (a + 1 - b) % 2) * 4 + z * 2 + c,
        "z": s + 2 - 4 * z,
    }
    core = s + 1 - 2 * c

    def gene_of(d):
        return {"gene": (g + d) % N_GENE}

    def sample_of(d):
        return {"sample": (s + d) % N_SAMPLE}

    def quarter_of(d):
        return (g + N_GENE - d) % N_GENE

    def load(d, h):
        source = pl.ds(pl.multiple_of(quarter_of(d) * quarter + h * half, half), half)
        target = pl.ds(pl.multiple_of(d * quarter + h * half, half), half)
        return pltpu.make_async_copy(expr_hbm.at[source, :], e_v.at[target, :], e_sem.at[d, h])

    def load_dosage(d):
        source = pl.ds(pl.multiple_of(quarter_of(d) * quarter, quarter), quarter)
        return pltpu.make_async_copy(dos_hbm.at[source, :], d_v.at[pl.ds(d * quarter, quarter), :], d_sem.at[d])

    def remote(src, dst, recv, device):
        return pltpu.make_async_remote_copy(
            src_ref=src, dst_ref=dst, send_sem=sent, recv_sem=recv, device_id=device, device_id_type=MESH
        )

    sig_copy = pltpu.make_async_copy(sig_hbm, sig_ref, i_sem.at[0])
    prof_copy = pltpu.make_async_copy(prof_hbm, prof_ref, i_sem.at[1])
    sig_copy.start()
    prof_copy.start()
    for h in range(2):
        load(1, h).start()

    barrier = pltpu.get_barrier_semaphore()
    for d in range(1, N_GENE):
        pl.semaphore_signal(barrier, inc=1, device_id=gene_of(d), device_id_type=MESH)
    for d in range(1, N_SAMPLE):
        pl.semaphore_signal(barrier, inc=1, device_id=sample_of(d), device_id_type=MESH)

    n_sig = sig_ref.shape[1]
    sig_sc[...] = jnp.full(sig_sc.shape, -1, jnp.int32)
    sig_copy.wait()
    prof_copy.wait()
    for d in (2, 3, 0):
        for h in range(2):
            load(d, h).start()
    for d in range(N_GENE):
        load_dosage(d).start()
    sig_sc[0:1, 0:n_sig] = sig_ref[...]
    cols = []
    for t in range(sig_sc.shape[1] // 128):
        line = sig_sc[0:1, 128 * t : 128 * t + 128].astype(F32)
        cols.append(jnp.transpose(jnp.broadcast_to(line, (128, 128))))
    lane = lax.broadcasted_iota(jnp.int32, (128, 128), 1) + g * g_dev
    m_sc[...] = jnp.zeros(m_sc.shape, F32)
    for t in range(n_tiles):
        ids = (lane + 128 * t).astype(F32)
        hit = jnp.zeros((128, 128), F32)
        for column in cols:
            hit = jnp.where(column == ids, 1.0, hit)
        member = jnp.max(hit, axis=0, keepdims=True)
        m_sc[0:types, 128 * t : 128 * t + 128] = prof_ref[:, 128 * t : 128 * t + 128] * member
    masked = m_sc[...]
    gsnd[...] = jnp.zeros(gsnd.shape, F32)
    gsnd[:, 0:8] = lax.dot_general(masked, masked, NT, precision=HIGH, preferred_element_type=F32)
    top = masked.astype(BF16).astype(F32)
    rest = masked - top
    mid = rest.astype(BF16).astype(F32)
    m3 = jnp.concatenate([top, mid, rest - mid], axis=0).astype(BF16)

    def gram_copy(d):
        return remote(gsnd, grcv.at[d - 1], g_r.at[d - 1], gene_of(d))

    def rhs_copy(d):
        return remote(rsnd.at[d], rrcv.at[d - 1], x_r.at[d - 1], gene_of(d))

    def rhs_quarter(i, carry):
        d = N_GENE - 1 - i
        at = (N_GENE - d) % N_GENE
        for h in range(2):
            load(at, h).wait()
        for h in range(2):
            rows = pl.ds(pl.multiple_of(at * quarter + h * half, half), half)
            part = lax.dot_general(m3, e_v[rows, :], NT, preferred_element_type=F32)
            rsnd[d, :, h * half : (h + 1) * half] = part[0:8] + part[8:16] + part[16:24]

        @pl.when(i == 0)
        def _():
            pl.semaphore_wait(barrier, N_GENE - 1 + N_SAMPLE - 1)
            for peer in range(1, N_GENE):
                gram_copy(peer).start()

        @pl.when(d > 0)
        def _():
            rhs_copy(d).start()

        return carry

    lax.fori_loop(0, N_GENE, rhs_quarter, 0)

    for d in range(N_GENE):
        load_dosage(d).wait()
    for i in range(s_dev // 128):
        piece = d_v[128 * i : 128 * i + 128, :].astype(F32).astype(BF16)
        d_t[:, 128 * i : 128 * i + 128] = jnp.transpose(piece)
    corr_sc[...] = jnp.zeros(corr_sc.shape, F32)
    pp_sc[...] = jnp.zeros(pp_sc.shape, F32)
    gram = gsnd[:, 0:8]
    for d in range(1, N_GENE):
        gram_copy(d).wait_recv()
        gram = gram + grcv[d - 1, :, 0:8]
    factor = ldl(gram)
    for d in (3, 2, 1):
        rhs_copy(d).wait_recv()
    pbuf[g] = solve(factor, rsnd[0] + rrcv[2] + rrcv[1] + rrcv[0])

    def props_copy(d):
        return remote(pbuf.at[g], pbuf.at[g], p_r.at[d - 1], gene_of(d))

    for d in (2, 1, 3):
        props_copy(d).start()

    def span_of(d):
        return slice(d * quarter, (d + 1) * quarter)

    def design(d):
        props = pbuf[quarter_of(d)]
        props_ref[:, pl.ds(pl.multiple_of(quarter_of(d) * quarter, quarter), quarter)] = props[0:types]
        top = props.astype(BF16).astype(F32)
        des[896:912, span_of(d)] = jnp.concatenate([top, props - top], axis=0).astype(BF16)
        for k in range(types):
            lo, hi = [part for part in PARTS if part[0] <= k < part[1]][0]
            wide = jnp.broadcast_to(top[k : k + 1, :], (16, quarter)).astype(BF16)
            for bb in range(2):
                for aa in range(2):
                    for zz in range(2):
                        source = ((2 * bb + (aa + bb) % 2) * 2 + zz) * 16
                        target = lo * 128 + (((bb * 2 + aa) * 2 + zz) * (hi - lo) + k - lo) * 16
                        des[target : target + 16, span_of(d)] = d_t[source : source + 16, span_of(d)] * wide

    def small_term(d):
        span = pl.ds(pl.multiple_of(d * quarter, quarter), quarter)
        props = pbuf[quarter_of(d)]
        top = props.astype(BF16).astype(F32)
        highs, lows = [], []
        for k in range(types):
            weight = jnp.broadcast_to(top[k : k + 1, :], (8, quarter)) * props
            high = weight.astype(BF16).astype(F32)
            highs.append(high)
            lows.append(weight - high)
        w = jnp.concatenate(highs + lows, axis=0).astype(BF16)
        corr = lax.dot_general(d_t[:, span], w, NT, preferred_element_type=F32)
        both = des[896:912, span]
        pp = lax.dot_general(both, both, NT, preferred_element_type=F32)
        corr_sc[:, 0 : 16 * types] += corr
        pp_sc[:, 0:16] += pp[0:8] + pp[8:16]

    def term(n, first):
        columns = pl.ds(pl.multiple_of(n * n_cols, n_cols), n_cols)
        span = slice(0, quarter) if first else slice(quarter, s_dev)
        value = jnp.dot(des[:, span], e_v[span, columns], preferred_element_type=F32)
        for part, (lo, hi) in enumerate(PARTS):
            body = value[128 * lo : 128 * hi].reshape(acc[part].shape[1:])
            acc[part][n] = body if first else acc[part][n] + body
        tail = value[896:904] + value[904:912]
        py_sc[n] = tail if first else py_sc[n] + tail

    def core_copy(n, part):
        return remote(
            acc[part].at[n, :, :, :, :, 1 - c], rc[part].at[n], c_r.at[n, part], {"sample": core}
        )

    def halving(n, part, step):
        axes = ORDERS[n][part]
        kept = {axis: place[axis] for axis in axes[:step]}
        axis = axes[step]

        def block(fixed):
            return (n,) + tuple(fixed.get(name, slice(None)) for name in "baz") + (slice(None), c)

        landing = ((r1, r2, r3)[step])[part].at[n]
        copy = remote(
            acc[part].at[block({**kept, axis: 1 - place[axis]})],
            landing,
            h_r.at[n, part, step],
            {"sample": other[axis]},
        )
        return copy, block({**kept, axis: place[axis]}), landing

    def advance(n, part, step):
        if step < 0:
            core_copy(n, part).wait_recv()
            acc[part][n, :, :, :, :, c] += rc[part][n]
        else:
            copy, kept, landing = halving(n, part, step)
            copy.wait_recv()
            acc[part][kept] += landing[...]
        halving(n, part, step + 1)[0].start()

    def tile_copy(d):
        return remote(tsrc.at[(s + d) % N_SAMPLE], trcv.at[d], t_r, sample_of(d))

    def spread_copy(d):
        return remote(tbuf.at[0], tbuf.at[d], u_r, sample_of(d))

    def start_tiles(d, carry):
        tile_copy(d).start()
        return carry

    def wait_tiles(buffer, recv):
        remote(tsrc.at[1:N_SAMPLE], buffer.at[1:N_SAMPLE], recv, sample_of(1)).wait_recv()

    def start_spread(d, carry):
        spread_copy(d).start()
        return carry

    spot = lax.broadcasted_iota(jnp.int32, (8, 128), 1)
    n_kj = 8 * types

    def send_tiles():
        pp = pp_sc[...]
        pp = pltpu.roll(pp + pltpu.roll(pp, 120, 1), n_kj, 1)
        for i in range(N_SAMPLE):
            corr = corr_sc[8 * i : 8 * i + 8, :]
            corr = corr + pltpu.roll(corr, 128 - n_kj, 1)
            at = 64 * i
            py = py_sc[at // n_cols, :, at % n_cols // 128 * 128 : at % n_cols // 128 * 128 + 128]
            if i % 2 == 0:
                py = pltpu.roll(py, 64, 1)
            tsrc[i] = jnp.where(spot < n_kj, corr, jnp.where(spot < 64, pp, py))
        lax.fori_loop(1, N_SAMPLE, start_tiles, 0)

    def spread_tiles():
        wait_tiles(trcv, t_r)
        total = tsrc[s]
        for d in range(1, N_SAMPLE):
            total = total + trcv[d]
        tbuf[0] = total
        lax.fori_loop(1, N_SAMPLE, start_spread, 0)
        corr_sc[0:8, :] = total

    def factor_pp():
        total = corr_sc[0:8, :]
        inv, inv_t, diag = ldl(pltpu.roll(total, 128 - n_kj, 1)[:, 0:8])
        fac_sc[0, :, 0:8] = inv
        fac_sc[1, :, 0:8] = inv_t
        fac_sc[2, :, 0:1] = diag

    def solve_coef():
        wait_tiles(tbuf, u_r)
        factor = fac_sc[0, :, 0:8], fac_sc[1, :, 0:8], fac_sc[2, :, 0:1]
        own = [tbuf[(s + N_SAMPLE - i) % N_SAMPLE] for i in range(N_SAMPLE)]
        tiles = [jnp.where(spot < 64, pltpu.roll(own[2 * i], 64, 1), own[2 * i + 1]) for i in range(n_tiles)]
        m_sc[...] = solve(factor, jnp.concatenate(tiles, axis=1))

    def finish(n, part):
        corr = corr_sc[0:8, :]
        coef = m_sc[:, n * n_cols : (n + 1) * n_cols]
        copy, kept, landing = halving(n, part, 2)
        copy.wait_recv()
        value = acc[part][kept] + landing[...]
        for k in range(*PARTS[part]):
            out = value[k - PARTS[part][0]]
            for j in range(types):
                out = out - corr[:, 8 * k + j : 8 * k + j + 1] * coef[j : j + 1, :]
            out = out * scale
            for i in range(per_chunk):
                mix[n * per_chunk + i, pl.ds(k, 8, stride=types), :] = out[:, 128 * i : 128 * i + 128]

    design(0)

    def own(n, carry):
        term(n, True)
        return carry

    lax.fori_loop(0, N_CHUNK, own, 0)
    small_term(0)
    for d in (1, 3, 2):
        props_copy(d).wait_recv()
        design(d)

    def others(n, carry):
        term(n, False)
        for part in range(3):
            core_copy(n, part).start()

        @pl.when(n > 0)
        def _():
            small_term(n)

        @pl.when(n == N_CHUNK - 1)
        def _():
            advance(0, 0, 0)
            advance(0, 1, 0)
            send_tiles()

        for chunk in range(1, N_CHUNK):
            @pl.when(n == chunk)
            def _(chunk=chunk):
                for part in range(3):
                    advance(chunk - 1, part, -1)

        return carry

    lax.fori_loop(0, N_CHUNK, others, 0)
    for event in AFTER:
        if event == "spread":
            spread_tiles()
        elif event == "factor":
            factor_pp()
        else:
            advance(*event)
    solve_coef()
    left = [3] * N_CHUNK
    for n, part in LAST:
        finish(n, part)
        left[n] -= 1
        if left[n] == 0:
            for i in range(n * per_chunk, (n + 1) * per_chunk):
                inter_ref[:, 128 * i : 128 * i + 128] = mix[i]

    for d in range(1, N_GENE):
        gram_copy(d).wait_send()
        rhs_copy(d).wait_send()
        props_copy(d).wait_send()
    for n in range(N_CHUNK):
        for part in range(3):
            core_copy(n, part).wait_send()
            for step in range(3):
                halving(n, part, step)[0].wait_send()

    def drain_tiles(d, carry):
        tile_copy(d).wait_send()
        spread_copy(d).wait_send()
        return carry

    lax.fori_loop(1, N_SAMPLE, drain_tiles, 0)


def store(inter_ref, props_ref, inter_out, props_out, sem):
    copies = (
        pltpu.make_async_copy(inter_ref, inter_out, sem.at[0]),
        pltpu.make_async_copy(props_ref, props_out, sem.at[1]),
    )
    for copy in copies:
        copy.start()
    for copy in copies:
        copy.wait()


def local(expression, profile, dosage, signature):
    s_dev, g_dev = expression.shape
    v_dev = dosage.shape[1]
    types = profile.shape[1]
    quarter, n_cols = s_dev // N_GENE, g_dev // N_CHUNK
    scale = 1.0 / math.sqrt(s_dev * N_SAMPLE)
    sig_cols = -(-signature.shape[0] // 128) * 128
    sizes = [hi - lo for lo, hi in PARTS]
    vmem, dma = pltpu.VMEM, pltpu.SemaphoreType.DMA
    inter, props_t = pl.pallas_call(
        functools.partial(kernel, scale),
        out_shape=(
            vmem((v_dev * types // N_SAMPLE, g_dev), F32),
            vmem((types, s_dev), F32),
        ),
        in_specs=[
            pl.BlockSpec(memory_space=pl.ANY),
            pl.BlockSpec(memory_space=pl.ANY),
            pl.BlockSpec(memory_space=pl.ANY),
            pl.BlockSpec(memory_space=pl.ANY),
        ],
        out_specs=(pl.BlockSpec(memory_space=pltpu.VMEM), pl.BlockSpec(memory_space=pltpu.VMEM)),
        scratch_shapes=[
            vmem((s_dev, g_dev), BF16),
            vmem((s_dev, v_dev), jnp.int32),
            vmem((v_dev, s_dev), BF16),
            vmem((v_dev * types + 16, s_dev), BF16),
            vmem((1, signature.shape[0]), jnp.int32),
            vmem((types, g_dev), F32),
            vmem((1, sig_cols), jnp.int32),
            vmem((8, g_dev), F32),
            [vmem((N_CHUNK, 2, 2, 2, k, 2, 8, n_cols), F32) for k in sizes],
            [vmem((N_CHUNK, 2, 2, 2, k, 8, n_cols), F32) for k in sizes],
            [vmem((N_CHUNK, 2, 2, k, 8, n_cols), F32) for k in sizes],
            [vmem((N_CHUNK, 2, k, 8, n_cols), F32) for k in sizes],
            [vmem((N_CHUNK, k, 8, n_cols), F32) for k in sizes],
            vmem((N_GENE, 8, quarter), F32),
            vmem((N_GENE, 8, quarter), F32),
            vmem((N_GENE - 1, 8, quarter), F32),
            vmem((8, 128), F32),
            vmem((N_GENE - 1, 8, 128), F32),
            vmem((v_dev, 128), F32),
            vmem((8, 128), F32),
            vmem((N_CHUNK, 8, n_cols), F32),
            vmem((3, 8, 128), F32),
            vmem((N_SAMPLE, 8, 128), F32),
            vmem((N_SAMPLE, 8, 128), F32),
            vmem((N_SAMPLE, 8, 128), F32),
            vmem((g_dev // 128, 8 * types, 128), F32),
            dma((N_GENE, 2)),
            dma((N_GENE,)),
            dma((2,)),
            dma,
            dma((N_GENE - 1,)),
            dma((N_GENE - 1,)),
            dma((N_GENE - 1,)),
            dma((N_CHUNK, 3)),
            dma((N_CHUNK, 3, 3)),
            dma,
            dma,
        ],
        compiler_params=pltpu.CompilerParams(
            collective_id=0, has_side_effects=True, vmem_limit_bytes=VMEM_BYTES
        ),
        name="eqtl",
    )(signature.reshape(1, -1), profile.T, expression, dosage)
    inter, props_t = pl.pallas_call(
        store,
        out_shape=(
            jax.ShapeDtypeStruct(inter.shape, F32),
            jax.ShapeDtypeStruct(props_t.shape, F32),
        ),
        in_specs=[pl.BlockSpec(memory_space=pltpu.VMEM)] * 2,
        out_specs=(pl.BlockSpec(memory_space=pl.ANY), pl.BlockSpec(memory_space=pl.ANY)),
        scratch_shapes=[dma((2,))],
        compiler_params=pltpu.CompilerParams(vmem_limit_bytes=8 * 1024 * 1024),
        name="store",
    )(inter, props_t)
    return inter, props_t.T


def solution(mesh):
    placed = (P("sample", "gene"), P("gene", None), P("sample", "variant"), P())
    return jax.shard_map(
        local,
        mesh=mesh,
        in_specs=placed,
        out_specs=(P(("variant", "sample"), "gene"), P("sample", None)),
        check_vma=False,
    )
```
